32 devices in a mesh: doc: 2 (over core), coarse: 2 (over x), fine: 8 (over z, y).
Axes of the slice: x: 2, y: 2, z: 4, core: 2. Of those that a mesh axis runs over, the one named last changes fastest.
Arguments:
- q_light: bfloat16 [2, 2048, 1024], P('doc', ('coarse', 'fine')), may hold values from -8 to 8
- k_light: bfloat16 [2, 2048, 1024], P('doc', ('coarse', 'fine')), may hold values from -8 to 8
- v_light: bfloat16 [2, 2048, 1024], P('doc', ('coarse', 'fine')), may hold values from -6 to 6
- q_heavy: bfloat16 [2, 2048, 1024], P('doc', ('coarse', 'fine')), may hold values from -8 to 8
- k_heavy: bfloat16 [2, 2048, 1024], P('doc', ('coarse', 'fine')), may hold values from -8 to 8
- v_heavy: bfloat16 [2, 2048, 1024], P('doc', ('coarse', 'fine')), may hold values from -6 to 6
- enc_kv: bfloat16 [2, 2048, 128], P('doc', ('coarse', 'fine')), may hold values from -8 to 8
- dec_queries: bfloat16 [2, 512, 1024], P('doc'), may hold values from -8 to 8
- query_ids: int32 [2, 16], P('doc'), may hold values from 0 to 15, as said below
- key_ids: int32 [2, 16], P('doc'), may hold values from 0 to 15, as said below
Outputs:
- encoded: bfloat16 [2, 2048, 1024], P('doc', ('coarse', 'fine'))
- decoded: bfloat16 [2, 512, 1024], P('doc')
The draws below stay inside these ranges and needn't reach their ends.
Inputs may be any that keep to these rules, and one draw needn't show every extreme that they name: `query_ids`: for each document and each c below the number of coarse groups, entries c * 8 to (c + 1) * 8 - 1 are distinct block numbers among blocks c * 8 to (c + 1) * 8 - 1 (so every block of the group is listed), and entry c * 8 + f is the block assigned to the f-th device of that group. `key_ids`: for each document and each c below the number of coarse groups, entries c * 8 to (c + 1) * 8 - 1 are distinct block numbers among blocks c * 8 * 1 to (c + 1) * 8 - 1.
All inputs are finite; a program needn't handle non-finite values.
Results may differ from the reference program's by a relative error of at most 0.009.
Values may be sent and summed in bfloat16 or wider, within the bound.
A program may use at most 384 MiB of HBM per device.

```python
import jax
import jax.numpy as jnp
from jax import lax

HEADS = 16
HEAD = 64
ROUTED_BLOCK = 128
KGRP = 8
DEC = 512
TOK_DEV = 128
DOCS = 2
DOCUMENT_TOKENS = 2048
N_COARSE = 2
N_FINE = 8


def choose_blocks(key, count):
    per_group = N_FINE * (TOK_DEV // ROUTED_BLOCK)
    blk_dev = TOK_DEV // ROUTED_BLOCK

    def one_group(sub):
        leading_entry, second, third = jax.random.split(sub, 3)
        fullest = jax.random.randint(leading_entry, (), 0, N_FINE)
        scores = jax.random.permutation(second, per_group).astype(jnp.int32)
        local = jnp.arange(per_group, dtype=jnp.int32)
        forced = (local // blk_dev == fullest) & (local % blk_dev < min(blk_dev, count))
        scores = jnp.where(forced, scores + per_group, scores)
        order = jnp.argsort(-scores, stable=True)
        chosen = order[:count].astype(jnp.int32)
        return jax.random.permutation(third, chosen)
    keys = jax.random.split(key, DOCS * N_COARSE)
    picks = jax.vmap(one_group)(keys).reshape(DOCS, N_COARSE, count)
    block_offsets = jnp.arange(N_COARSE, dtype=jnp.int32) * per_group
    return (picks + block_offsets[None, :, None]).reshape(DOCS, N_COARSE * count).astype(jnp.int32)


def draw_query_ids(key, part):
    return choose_blocks(jax.random.fold_in(key, 11), N_FINE)


def draw_key_ids(key, part):
    return choose_blocks(jax.random.fold_in(key, 23), KGRP)


def drawn(key, shape):
    return jnp.clip(jax.random.normal(key, shape, jnp.float32), -6.0, 6.0)


def draw_q_light(key, part):
    field_key = jax.random.fold_in(key, 31)
    shape = (DOCS, DOCUMENT_TOKENS, HEADS * HEAD)
    return drawn(field_key, shape).astype(jnp.bfloat16)


def draw_k_light(key, part):
    field_key = jax.random.fold_in(key, 37)
    shape = (DOCS, DOCUMENT_TOKENS, HEADS * HEAD)
    return drawn(field_key, shape).astype(jnp.bfloat16)


def draw_q_heavy(key, part):
    field_key = jax.random.fold_in(key, 41)
    shape = (DOCS, DOCUMENT_TOKENS, HEADS * HEAD)
    return drawn(field_key, shape).astype(jnp.bfloat16)


def draw_k_heavy(key, part):
    field_key = jax.random.fold_in(key, 43)
    shape = (DOCS, DOCUMENT_TOKENS, HEADS * HEAD)
    return jnp.clip(3.0 * jax.random.normal(field_key, shape, jnp.float32), -8.0, 8.0).astype(jnp.bfloat16)


def draw_enc_kv(key, part):
    field_key = jax.random.fold_in(key, 47)
    shape = (DOCS, DOCUMENT_TOKENS, 2 * HEAD)
    return drawn(field_key, shape).astype(jnp.bfloat16)


def draw_dec_queries(key, part):
    field_key = jax.random.fold_in(key, 53)
    shape = (DOCS, DEC, HEADS * HEAD)
    return drawn(field_key, shape).astype(jnp.bfloat16)


def steps_of(own_key, shape, shards, low, largest):
    level, own = 1.0, jax.random.fold_in(own_key, 6)
    for axis_at, shards_of in shards:
        draws = jnp.exp(jax.random.uniform(jax.random.fold_in(own, axis_at), (shards_of,), jnp.float32, low / len(shards), largest / len(shards)))
        level = level * jnp.repeat(draws, shape[axis_at] // shards_of).reshape([-1 if axis == axis_at else 1 for axis in range(len(shape))])
    return level


def bell_draw(key, shape, deviation, most, shards=(), kind=jnp.bfloat16):
    entries = jax.random.normal(key, shape, jnp.float32) * deviation
    if len(shards) > 0:
        entries = steps_of(key, shape, shards, -0.22, 0.18) * entries
    return jnp.clip(entries, min=-most, max=most).astype(kind)


def setup_inputs(seed: int = 0) -> dict:
    splits = jax.random.split(jax.random.key(seed), 11)
    return {
        "q_light": draw_q_light(jax.random.fold_in(splits[10], 71), 0),
        "k_light": draw_k_light(jax.random.fold_in(splits[10], 71), 0),
        "v_light": bell_draw(splits[2], (DOCS, DOCUMENT_TOKENS, HEADS * HEAD), 1.0, 6.0, ((0, 2), (1, 16))),
        "q_heavy": draw_q_heavy(jax.random.fold_in(splits[10], 71), 0),
        "k_heavy": draw_k_heavy(jax.random.fold_in(splits[10], 71), 0),
        "v_heavy": bell_draw(splits[5], (DOCS, DOCUMENT_TOKENS, HEADS * HEAD), 1.0, 6.0, ((0, 2), (1, 16))),
        "enc_kv": draw_enc_kv(jax.random.fold_in(splits[10], 71), 0),
        "dec_queries": draw_dec_queries(jax.random.fold_in(splits[10], 71), 0),
        "query_ids": draw_query_ids(jax.random.fold_in(splits[10], 71), 0),
        "key_ids": draw_key_ids(jax.random.fold_in(splits[10], 71), 0),
    }


def attend(query, keys, value_rows, mask):
    rows = query.shape[0]
    count = keys.shape[0]
    heads = query.shape[1] // HEAD
    qh = query.reshape(rows, heads, HEAD).transpose(1, 0, 2)
    kh = keys.reshape(count, heads, HEAD).transpose(1, 0, 2)
    vh = value_rows.reshape(count, heads, HEAD).transpose(1, 0, 2)

    def one_head(triple):
        qa, ka, va = triple
        scores = jnp.dot(qa, ka.T, preferred_element_type=jnp.float32) * (HEAD ** -0.5)
        if mask is not None:
            scores = jnp.where(mask, scores, jnp.float32(-1e30))
        peak = jnp.max(scores, axis=1, keepdims=True)
        weights = jnp.exp(scores - peak)
        weights = (weights / jnp.sum(weights, axis=1, keepdims=True)).astype(jnp.bfloat16)
        return jnp.dot(weights, va, preferred_element_type=jnp.float32)

    out = lax.map(one_head, (qh, kh, vh))
    return out.transpose(1, 0, 2).reshape(rows, heads * HEAD)


def light_part(query, keys, value_rows):
    length = query.shape[0]
    width = query.shape[1]
    kpad = jnp.pad(keys, ((ROUTED_BLOCK, ROUTED_BLOCK), (0, 0)))
    padded_values = jnp.pad(value_rows, ((ROUTED_BLOCK, ROUTED_BLOCK), (0, 0)))

    def one_block(index):
        leading_entry = index * ROUTED_BLOCK
        qb = lax.dynamic_slice_in_dim(query, leading_entry, ROUTED_BLOCK)
        kb = lax.dynamic_slice_in_dim(kpad, leading_entry, 3 * ROUTED_BLOCK)
        value_block = lax.dynamic_slice_in_dim(padded_values, leading_entry, 3 * ROUTED_BLOCK)
        qpos = leading_entry + jnp.arange(ROUTED_BLOCK, dtype=jnp.int32)
        kpos = leading_entry - ROUTED_BLOCK + jnp.arange(3 * ROUTED_BLOCK, dtype=jnp.int32)
        mask = (jnp.abs(qpos[:, None] - kpos[None, :]) <= ROUTED_BLOCK - 1) & (kpos[None, :] >= 0) & (kpos[None, :] < length)
        return attend(qb, kb, value_block, mask)

    out = lax.map(one_block, jnp.arange(length // ROUTED_BLOCK, dtype=jnp.int32))
    return out.reshape(length, width)


def heavy_part(query, keys, value_rows, qids, kids):
    length, width = query.shape
    nblk = length // ROUTED_BLOCK
    qblocks = jnp.take(query.reshape(nblk, ROUTED_BLOCK, width), qids.astype(jnp.int32), axis=0)
    kall = jnp.take(keys.reshape(nblk, ROUTED_BLOCK, width), kids.astype(jnp.int32), axis=0).reshape(-1, width)
    vall = jnp.take(value_rows.reshape(nblk, ROUTED_BLOCK, width), kids.astype(jnp.int32), axis=0).reshape(-1, width)
    res = lax.map(lambda qb: attend(qb, kall, vall, None).astype(jnp.bfloat16), qblocks)
    full = jnp.zeros((nblk, ROUTED_BLOCK, width), jnp.bfloat16).at[qids.astype(jnp.int32)].set(res)
    return full.reshape(length, width)


def decoder_part(queries, enc):
    count = queries.shape[0]
    heads = queries.shape[1] // HEAD
    kenc = enc[:, :HEAD]
    venc = enc[:, HEAD:]
    qh = queries.reshape(count, heads, HEAD).transpose(1, 0, 2)

    def one_head(qa):
        scores = jnp.dot(qa, kenc.T, preferred_element_type=jnp.float32) * (HEAD ** -0.5)
        peak = jnp.max(scores, axis=1, keepdims=True)
        weights = jnp.exp(scores - peak)
        total = jnp.sum(weights, axis=1, keepdims=True)
        return jnp.dot(weights.astype(jnp.bfloat16), venc, preferred_element_type=jnp.float32) / total

    out = lax.map(one_head, qh)
    return out.transpose(1, 0, 2).reshape(count, heads * HEAD).astype(jnp.bfloat16)


def reference(q_light, k_light, v_light, q_heavy, k_heavy, v_heavy, enc_kv, dec_queries, query_ids, key_ids):
    encoded = []
    decoded = []
    for doc in range(DOCS):
        light = light_part(q_light[doc], k_light[doc], v_light[doc])
        heavy = heavy_part(q_heavy[doc], k_heavy[doc], v_heavy[doc], query_ids[doc], key_ids[doc])
        encoded.append((light + heavy.astype(jnp.float32)).astype(jnp.bfloat16))
        decoded.append(decoder_part(dec_queries[doc], enc_kv[doc]))
    return jnp.stack(encoded), jnp.stack(decoded)
```

```python
import functools

import jax
import jax.numpy as jnp
from jax import lax
from jax.experimental import pallas as pl
from jax.experimental.pallas import tpu as pltpu
from jax.sharding import PartitionSpec as P

HEAD = 64
PAIR = 2 * HEAD
ROUTED_BLOCK = 128
LOW = 2
MESH = pl.DeviceIdType.MESH
NEG = -1e30


def dot_t(a, b):
    return lax.dot_general(a, b, (((1,), (1,)), ((), ())), preferred_element_type=jnp.float32)


def dot(a, b):
    return jnp.dot(a, b, preferred_element_type=jnp.float32)


def stacked_pair(q, low_half):
    q = q * jnp.asarray(HEAD ** (-0.5), q.dtype)
    zero = jnp.zeros_like(q)
    return jnp.concatenate([jnp.where(low_half, q, zero), jnp.where(low_half, zero, q)], axis=0)


def flip(v, d, n):
    out, bit = 0, 1
    while bit < n:
        if isinstance(d, int):
            on = (d // bit) % 2
        else:
            on = lax.rem(lax.div(d, bit), 2)
        out = out + lax.rem(lax.div(v, bit) + on, 2) * bit
        bit *= 2
    return out


def kernel(dims, has_bias, *refs):
    n_coarse, n_fine, tokens, width, dec_rows = dims
    n_seq = n_coarse * n_fine
    n_q = n_fine // LOW
    n_kv = n_coarse * LOW
    n_pair_seq = n_seq // LOW
    half = n_fine // 2
    heads = width // HEAD
    pairs = heads // 2
    share = n_fine // pairs
    wide = width // LOW
    pairs_half = pairs // LOW
    refs = list(refs)
    ql, kl, vl, qh, kh, vh, enc, decq = refs[:8]
    bias_ref = refs[8] if has_bias else None
    (out, dec, encbuf, drows, dq, do, qbuf, kbuf, vbuf, acc, stat, osend, orecv,
     lq, lk, lv, lown, lsend, lrecv, band,
     load_s, enc_s, enc_r, ek_s, ek_r, q_s, q_r, k_s, k_r, v_s, v_r, kx_s, vx_s,
     x_s, x_r, h_s, h_r, o_s, o_r, lo_s, lo_r, dec_s, dec_r) = refs[8 + has_bias:]

    c = lax.axis_index("coarse")
    f = lax.axis_index("fine")
    here = c * n_fine + f
    me_q = lax.div(f, LOW)
    lo = lax.rem(f, LOW)
    me_kv = c * LOW + lo
    p = lax.div(f, share)
    s_me = lax.rem(f, share)
    hh = lax.div(f, half)
    g = lax.rem(f, half)
    two = lax.div(here, LOW)

    def remote(src, dst, ssem, rsem, device):
        return pltpu.make_async_remote_copy(
            src_ref=src, dst_ref=dst, send_sem=ssem, recv_sem=rsem,
            device_id=device, device_id_type=MESH,
        )

    def up(me, d, n):
        return lax.rem(me + d, n)

    def down(me, d, n):
        return lax.rem(me + n - d, n)

    def at(cc, ff):
        return {"coarse": cc, "fine": ff}

    def cols_of(pair):
        return pl.ds(pl.multiple_of(pair * PAIR, PAIR), PAIR)

    def side_of(which):
        return pl.ds(pl.multiple_of(which * wide, PAIR), wide)

    def loop(start, stop, body):
        def step(d, carry):
            body(d)
            return carry
        lax.fori_loop(start, stop, step, 0)

    loads = [
        pltpu.make_async_copy(enc, encbuf.at[me_kv, me_q], load_s.at[0]),
        pltpu.make_async_copy(kh.at[:, cols_of(p)], kbuf.at[c, f], load_s.at[1]),
        pltpu.make_async_copy(vh.at[:, cols_of(p)], vbuf.at[c, f], load_s.at[2]),
        pltpu.make_async_copy(qh.at[:, cols_of(p)], qbuf.at[p], load_s.at[3]),
        pltpu.make_async_copy(decq.at[c, g], drows, load_s.at[4]),
        pltpu.make_async_copy(kl.at[:, side_of(lo)], lk.at[1 + lo], load_s.at[5]),
        pltpu.make_async_copy(vl.at[:, side_of(lo)], lv.at[1 + lo], load_s.at[6]),
        pltpu.make_async_copy(ql.at[:, side_of(lo)], lq.at[lo], load_s.at[7]),
    ]
    for copy in loads:
        copy.start()

    barrier = pltpu.get_barrier_semaphore()

    def greet(d, carry):
        t = up(here, d, n_seq)
        pl.semaphore_signal(
            barrier, inc=1, device_id=at(lax.div(t, n_fine), lax.rem(t, n_fine)), device_id_type=MESH
        )
        return carry

    lax.fori_loop(1, n_seq, greet, 0)
    pl.semaphore_wait(barrier, n_seq - 1)

    def at_q(a):
        return at(c, a * LOW + lo)

    def at_kv(b):
        return at(lax.div(b, LOW), me_q * LOW + lax.rem(b, LOW))

    def enc_copy(d):
        return remote(enc, encbuf.at[me_kv, me_q], enc_s.at[d], enc_r.at[me_q], at_q(up(me_q, d, n_q)))

    def enc_arrival(d):
        src = down(me_q, d, n_q)
        return remote(enc, encbuf.at[me_kv, src], enc_s.at[d], enc_r.at[src], at_q(src))

    other = c * LOW + 1 - lo

    def enc_low():
        return remote(encbuf.at[me_kv], encbuf.at[me_kv], ek_s.at[0, 0], ek_r.at[me_kv], at_kv(other))

    def enc_far(d, relay):
        block = other if relay else me_kv
        peer = up(c, d, n_coarse) * LOW + lo
        return remote(encbuf.at[block], encbuf.at[block], ek_s.at[int(relay), d], ek_r.at[block], at_kv(peer))

    def enc_block(block):
        return remote(encbuf.at[block], encbuf.at[block], ek_s.at[0, 0], ek_r.at[block], at_kv(block))

    def q_copy(d):
        to = flip(p, d, pairs)
        return remote(qh.at[:, cols_of(to)], qbuf.at[p], q_s.at[d], q_r.at[p], at(c, to * share + s_me))

    def q_arrival(d):
        src = flip(p, d, pairs)
        return remote(qbuf.at[src], qbuf.at[src], q_s.at[d], q_r.at[src], at(c, src * share + s_me))

    def kv_copy(d):
        to = flip(f, d, n_fine)
        col = cols_of(lax.div(to, share))
        return (
            remote(kh.at[:, col], kbuf.at[c, f], k_s.at[d], k_r.at[c, f], at(c, to)),
            remote(vh.at[:, col], vbuf.at[c, f], v_s.at[d], v_r.at[c, f], at(c, to)),
        )

    def kv_block(cc, ff):
        return (
            remote(kbuf.at[cc, ff], kbuf.at[cc, ff], k_s.at[0], k_r.at[cc, ff], at(cc, ff)),
            remote(vbuf.at[cc, ff], vbuf.at[cc, ff], v_s.at[0], v_r.at[cc, ff], at(cc, ff)),
        )

    def kv_relay(d, e):
        src = flip(f, d, n_fine)
        peer = at(up(c, e, n_coarse), f)
        return (
            remote(kbuf.at[c, src], kbuf.at[c, src], kx_s.at[d, e], k_r.at[c, src], peer),
            remote(vbuf.at[c, src], vbuf.at[c, src], vx_s.at[d, e], v_r.at[c, src], peer),
        )

    def kv_forward(d):
        if d:
            for copy in kv_block(c, flip(f, d, n_fine)):
                copy.wait_recv()
        for e in range(1, n_coarse):
            for copy in kv_relay(d, e):
                copy.start()

    def o_copy(d):
        to = flip(p, d, pairs)
        return remote(osend.at[to], orecv.at[p], o_s.at[d], o_r.at[p], at(c, to * share + s_me))

    def o_arrival(d):
        src = flip(p, d, pairs)
        return remote(osend.at[src], orecv.at[src], o_s.at[d], o_r.at[src], at(c, src * share + s_me))

    mate = at(c, f + 1 - 2 * lo)

    def swap_copy():
        cols = side_of(1 - lo)
        return (
            remote(kl.at[:, cols], lk.at[1 + lo], x_s.at[0], x_r.at[0], mate),
            remote(vl.at[:, cols], lv.at[1 + lo], x_s.at[1], x_r.at[1], mate),
            remote(ql.at[:, cols], lq.at[lo], x_s.at[2], x_r.at[2], mate),
        )

    def swap_arrival():
        return (
            remote(lk.at[2 - lo], lk.at[2 - lo], x_s.at[0], x_r.at[0], mate),
            remote(lv.at[2 - lo], lv.at[2 - lo], x_s.at[1], x_r.at[1], mate),
            remote(lq.at[1 - lo], lq.at[1 - lo], x_s.at[2], x_r.at[2], mate),
        )

    def halo_copy(side):
        peer = jnp.clip(two + 2 * side - 1, 0, n_pair_seq - 1) * LOW + lo
        device = at(lax.div(peer, n_fine), lax.rem(peer, n_fine))
        slot = 3 - 3 * side
        return (
            remote(lk.at[1 + side], lk.at[slot], h_s.at[side, 0], h_r.at[side, 0], device),
            remote(lv.at[1 + side], lv.at[slot], h_s.at[side, 1], h_r.at[side, 1], device),
        )

    has_peer = [two > 0, two < n_pair_seq - 1]

    def light_back():
        return remote(lsend, lrecv, lo_s, lo_r, mate)

    bits = []
    bit = half // 2
    while bit:
        bits.append(bit)
        bit //= 2

    def dec_copy(block, k):
        mine = dec.at[c, block]
        if k < len(bits):
            peer = at(c, hh * half + flip(g, bits[k], half))
        else:
            peer = at(up(c, k - len(bits) + 1, n_coarse), f)
        return remote(mine, mine, dec_s.at[k, block], dec_r.at[c, block], peer)

    def dec_arrival(cc, block):
        part = dec.at[cc, block]
        return remote(part, part, dec_s.at[0, 0], dec_r.at[cc, block], at(cc, f))

    def dec_spread(block, first):
        for k in range(first, len(bits) + n_coarse - 1):
            dec_copy(block, k).start()

    def dec_stage(k):
        done = [0]
        for b in bits[:k]:
            done = done + [x + b for x in done]
        return [flip(g, x + bits[k], half) for x in done]

    def dec_forward(k):
        for block in dec_stage(k):
            dec_arrival(c, block).wait_recv()
            dec_spread(block, k + 1)

    for d in range(1, n_q):
        enc_copy(d).start()
    for d in range(1, pairs):
        q_copy(d).start()
    loads[1].wait()
    loads[2].wait()
    kv_forward(0)
    for d in range(1, n_fine):
        for copy in kv_copy(d):
            copy.start()
    for copy in swap_copy():
        copy.start()
    loads[5].wait()
    loads[6].wait()

    for side in range(2):
        @pl.when((lo == side) & has_peer[side])
        def _():
            for copy in halo_copy(side):
                copy.start()

    row = lax.broadcasted_iota(jnp.int32, (tokens, 3 * tokens), 0)
    col = lax.broadcasted_iota(jnp.int32, (tokens, 3 * tokens), 1)
    for b in range(LOW):
        pos = (two * LOW + b) * tokens + col - tokens
        seen = (jnp.abs(col - tokens - row) <= ROUTED_BLOCK - 1) & (pos >= 0) & (pos < n_seq * tokens)
        band[b] = jnp.where(seen, jnp.float32(0), jnp.float32(NEG))

    loads[4].wait()
    lane_d = lax.broadcasted_iota(jnp.int32, (dec_rows, PAIR), 1)
    for j in range(pairs):
        q = drows[:, j * PAIR:(j + 1) * PAIR].astype(jnp.float32) * (HEAD ** (-0.5))
        swapped = pltpu.roll(q, HEAD, 1)
        both = jnp.concatenate(
            [jnp.where(lane_d < HEAD, q, 0.0), jnp.where(lane_d < HEAD, swapped, 0.0)], axis=0
        )
        dq[2 * j * dec_rows:(2 * j + 2) * dec_rows, :] = both.astype(jnp.bfloat16)

    loads[0].wait()
    for d in range(1, n_q):
        enc_arrival(d).wait_recv()
    enc_low().start()
    for d in range(1, n_coarse):
        enc_far(d, False).start()
    enc_block(other).wait_recv()
    for d in range(1, n_coarse):
        enc_far(d, True).start()

    for d in range(1, half):
        kv_forward(d)

    for d in range(1, n_coarse):
        for part in range(LOW):
            enc_block(up(c, d, n_coarse) * LOW + part).wait_recv()

    d_total = heads * dec_rows
    d_chunk = min(256, d_total)

    def dec_step(i):
        rows = pl.ds(pl.multiple_of(i * d_chunk, d_chunk), d_chunk)
        kv = encbuf[...].reshape(n_seq * tokens, PAIR)
        s = dot_t(dq[rows, :], kv)
        e = jnp.exp(s - jnp.max(s, axis=1, keepdims=True))
        total = jnp.sum(e, axis=1, keepdims=True)
        do[rows, :] = dot(e.astype(jnp.bfloat16), kv) / total

    loop(0, d_total // d_chunk, dec_step)
    for j in range(pairs):
        even = do[2 * j * dec_rows:(2 * j + 1) * dec_rows, :]
        odd = do[(2 * j + 1) * dec_rows:(2 * j + 2) * dec_rows, :]
        dec[c, g, :, j * PAIR:(j + 1) * PAIR] = jnp.where(
            lane_d < HEAD, pltpu.roll(even, HEAD, 1), odd
        ).astype(jnp.bfloat16)
    dec_spread(g, 0)

    low_half = lax.broadcasted_iota(jnp.int32, (tokens, PAIR), 1) < HEAD
    lane_2 = lax.broadcasted_iota(jnp.int32, (2 * tokens, PAIR), 1)
    keys = n_coarse * half * tokens

    def heavy_scores(j, part):
        q = stacked_pair(qbuf[j], low_half)
        s = dot_t(q, kbuf[:, pl.ds(part * half, half)].reshape(keys, PAIR))
        if has_bias:
            s = s + bias_ref[part, 0:1, :]
        return s

    def heavy_values(part):
        return vbuf[:, pl.ds(part * half, half)].reshape(keys, PAIR)

    def heavy_first(j):
        s = heavy_scores(j, hh)
        peak = jnp.max(s, axis=1, keepdims=True)
        e = jnp.exp(s - peak)
        total = jnp.sum(e, axis=1, keepdims=True)
        acc[j] = dot(e.astype(jnp.bfloat16), heavy_values(hh))
        stat[j] = jnp.where(lane_2 == 0, peak, total)

    def heavy_second(j):
        s = heavy_scores(j, 1 - hh)
        before = stat[j, :, 0:1]
        peak = jnp.maximum(before, jnp.max(s, axis=1, keepdims=True))
        e = jnp.exp(s - peak)
        keep = jnp.exp(before - peak)
        total = stat[j, :, 1:2] * keep + jnp.sum(e, axis=1, keepdims=True)
        o = (acc[j] * keep + dot(e.astype(jnp.bfloat16), heavy_values(1 - hh))) / total
        return jnp.where(low_half, o[:tokens], o[tokens:]).astype(jnp.bfloat16)

    loads[3].wait()
    for d in range(1, pairs):
        q_arrival(d).wait_recv()
    for e in range(1, n_coarse):
        for i in range(half):
            for copy in kv_block(up(c, e, n_coarse), hh * half + i):
                copy.wait_recv()
    per = max(1, pairs // half)
    done = 0
    for r in range(half):
        stop = pairs if r == half - 1 else min(pairs, done + per)
        loop(done, stop, heavy_first)
        done = stop
        kv_forward(half + r)

    for k in range(len(bits) - 1):
        dec_forward(k)
    arrived = swap_arrival()
    arrived[0].wait_recv()
    arrived[1].wait_recv()
    for side in range(2):
        @pl.when((lo == 1 - side) & has_peer[side])
        def _():
            for copy in halo_copy(side):
                copy.start()

    for e in range(1, n_coarse):
        for i in range(half):
            for copy in kv_block(up(c, e, n_coarse), (1 - hh) * half + i):
                copy.wait_recv()

    def heavy_out(i):
        d = pairs - 1 - i
        j = flip(p, d, pairs)
        osend[j] = heavy_second(j)
        o_copy(d).start()

    loop(0, pairs - 1, heavy_out)
    orecv[p] = heavy_second(p)
    dec_forward(len(bits) - 1)

    arrived[2].wait_recv()
    loads[7].wait()
    for side in range(2):
        @pl.when(has_peer[side])
        def _():
            for copy in halo_copy(1 - side):
                copy.wait_recv()

        @pl.when(jnp.logical_not(has_peer[side]))
        def _():
            lk[3 * side] = jnp.zeros((tokens, wide), jnp.bfloat16)
            lv[3 * side] = jnp.zeros((tokens, wide), jnp.bfloat16)

    def light_of(b, j):
        cols = cols_of(j)
        q = stacked_pair(lq[b, :, cols], low_half)
        mask = band[b]
        s = dot_t(q, lk[pl.ds(b, 3), :, cols].reshape(3 * tokens, PAIR))
        s = s + jnp.concatenate([mask, mask], axis=0)
        e = jnp.exp(s - jnp.max(s, axis=1, keepdims=True))
        total = jnp.sum(e, axis=1, keepdims=True)
        o = dot(e.astype(jnp.bfloat16), lv[pl.ds(b, 3), :, cols].reshape(3 * tokens, PAIR)) / total
        return jnp.where(low_half, o[:tokens], o[tokens:])

    def light_away(j):
        lsend[:, cols_of(j)] = light_of(1 - lo, j).astype(jnp.bfloat16)

    def light_home(j):
        lown[:, cols_of(j)] = light_of(lo, j)

    loop(0, pairs_half, light_away)
    light_back().start()
    loop(0, pairs_half, light_home)

    for d in range(1, pairs):
        o_arrival(d).wait_recv()

    def join_home(j):
        pair = lo * pairs_half + j
        heavy = orecv[pair].astype(jnp.float32)
        out[:, cols_of(pair)] = (lown[:, cols_of(j)] + heavy).astype(jnp.bfloat16)

    def join_away(j):
        pair = (1 - lo) * pairs_half + j
        heavy = orecv[pair].astype(jnp.float32)
        out[:, cols_of(pair)] = (lrecv[:, cols_of(j)].astype(jnp.float32) + heavy).astype(jnp.bfloat16)

    loop(0, pairs_half, join_home)
    light_back().wait_recv()
    loop(0, pairs_half, join_away)

    for e in range(1, n_coarse):
        for block in range(half):
            dec_arrival(up(c, e, n_coarse), block).wait_recv()
    for d in range(1, n_q):
        enc_copy(d).wait_send()
    enc_low().wait_send()
    for d in range(1, n_coarse):
        enc_far(d, False).wait_send()
        enc_far(d, True).wait_send()
    for d in range(1, pairs):
        q_copy(d).wait_send()
        o_copy(d).wait_send()
    for d in range(n_fine):
        if d:
            for copy in kv_copy(d):
                copy.wait_send()
        for e in range(1, n_coarse):
            for copy in kv_relay(d, e):
                copy.wait_send()
    for copy in swap_copy():
        copy.wait_send()
    light_back().wait_send()
    for side in range(2):
        @pl.when(has_peer[side])
        def _():
            for copy in halo_copy(side):
                copy.wait_send()
    for k in range(len(bits) + n_coarse - 1):
        sent = [0]
        for b in bits[:k]:
            sent = sent + [x + b for x in sent]
        for x in sent:
            dec_copy(flip(g, x, half), k).wait_send()


def local(
    q_light, k_light, v_light, q_heavy, k_heavy, v_heavy, enc_kv, dec_queries, query_ids, key_ids
):
    _, tokens, width = q_light.shape
    n_coarse = lax.axis_size("coarse")
    n_fine = lax.axis_size("fine")
    n_seq = n_coarse * n_fine
    n_q = n_fine // LOW
    n_kv = n_coarse * LOW
    half = n_fine // 2
    heads = width // HEAD
    pairs = heads // 2
    count = dec_queries.shape[1]
    dec_rows = count // (n_coarse * half)
    n_bits = half.bit_length() - 1
    mine = dec_queries.reshape(n_coarse, half, dec_rows, width)
    args = [q_light[0], k_light[0], v_light[0], q_heavy[0], k_heavy[0], v_heavy[0], enc_kv[0], mine]
    has_bias = key_ids.shape[1] != n_seq
    keys = n_coarse * half * tokens
    if has_bias:
        blocks = jnp.arange(n_seq, dtype=jnp.int32).reshape(n_coarse, 2, half).transpose(1, 0, 2)
        listed = jnp.any(blocks[..., None] == key_ids[0], axis=-1).reshape(2, 1, n_coarse * half)
        bias = jnp.repeat(jnp.where(listed, 0.0, NEG).astype(jnp.float32), tokens, axis=2)
        args.append(jnp.broadcast_to(bias, (2, 8, keys)))
    bf16, f32 = jnp.bfloat16, jnp.float32
    dma = pltpu.SemaphoreType.DMA
    vmem = pl.BlockSpec(memory_space=pltpu.VMEM)
    hbm = pl.BlockSpec(memory_space=pltpu.HBM)
    wide = width // LOW
    encoded, decoded = pl.pallas_call(
        functools.partial(kernel, (n_coarse, n_fine, tokens, width, dec_rows), has_bias),
        out_shape=(
            jax.ShapeDtypeStruct((tokens, width), bf16),
            jax.ShapeDtypeStruct((n_coarse, half, dec_rows, width), bf16),
        ),
        in_specs=[hbm] * 8 + [vmem] * (len(args) - 8),
        out_specs=(vmem, vmem),
        scratch_shapes=[
            pltpu.VMEM((n_kv, n_q, tokens, PAIR), bf16),
            pltpu.VMEM((dec_rows, width), bf16),
            pltpu.VMEM((heads * dec_rows, PAIR), bf16),
            pltpu.VMEM((heads * dec_rows, PAIR), f32),
            pltpu.VMEM((pairs, tokens, PAIR), bf16),
            pltpu.VMEM((n_coarse, n_fine, tokens, PAIR), bf16),
            pltpu.VMEM((n_coarse, n_fine, tokens, PAIR), bf16),
            pltpu.VMEM((pairs, 2 * tokens, PAIR), f32),
            pltpu.VMEM((pairs, 2 * tokens, PAIR), f32),
            pltpu.VMEM((pairs, tokens, PAIR), bf16),
            pltpu.VMEM((pairs, tokens, PAIR), bf16),
            pltpu.VMEM((2, tokens, wide), bf16),
            pltpu.VMEM((4, tokens, wide), bf16),
            pltpu.VMEM((4, tokens, wide), bf16),
            pltpu.VMEM((tokens, wide), f32),
            pltpu.VMEM((tokens, wide), bf16),
            pltpu.VMEM((tokens, wide), bf16),
            pltpu.VMEM((2, tokens, 3 * tokens), f32),
            dma((8,)),
            dma((n_q,)), dma((n_q,)),
            dma((2, n_coarse)), dma((n_kv,)),
            dma((pairs,)), dma((pairs,)),
            dma((n_fine,)), dma((n_coarse, n_fine)),
            dma((n_fine,)), dma((n_coarse, n_fine)),
            dma((n_fine, n_coarse)), dma((n_fine, n_coarse)),
            dma((3,)), dma((3,)),
            dma((2, 2)), dma((2, 2)),
            dma((pairs,)), dma((pairs,)),
            dma, dma,
            dma((n_bits + n_coarse - 1, half)), dma((n_coarse, half)),
        ],
        compiler_params=pltpu.CompilerParams(
            collective_id=0, has_side_effects=True, vmem_limit_bytes=60 * 1024 * 1024
        ),
    )(*args)
    return encoded[None], decoded.reshape(1, count, width)


def solution(mesh):
    rows = P("doc", ("coarse", "fine"), None)
    placed = (rows,) * 7 + (P("doc", None, None), P("doc", None), P("doc", None))
    return jax.shard_map(
        local,
        mesh=mesh,
        in_specs=placed,
        out_specs=(rows, P("doc", None, None)),
        check_vma=False,
    )
```

```python
import functools

import jax
import jax.numpy as jnp
from jax import lax
from jax.experimental import pallas as pl
from jax.experimental.pallas import tpu as pltpu
from jax.sharding import PartitionSpec as P

HEAD = 64
PAIR = 2 * HEAD
ROUTED_BLOCK = 128
LOW = 2
MESH = pl.DeviceIdType.MESH
NEG = -1e30


def dot_t(a, b):
    return lax.dot_general(a, b, (((1,), (1,)), ((), ())), preferred_element_type=jnp.float32)


def dot(a, b):
    return jnp.dot(a, b, preferred_element_type=jnp.float32)


def stacked_pair(q, low_half):
    q = q * jnp.asarray(HEAD ** (-0.5), q.dtype)
    zero = jnp.zeros_like(q)
    return jnp.concatenate([jnp.where(low_half, q, zero), jnp.where(low_half, zero, q)], axis=0)


def flip(v, d, n):
    out, bit = 0, 1
    while bit < n:
        if isinstance(d, int):
            on = (d // bit) % 2
        else:
            on = lax.rem(lax.div(d, bit), 2)
        out = out + lax.rem(lax.div(v, bit) + on, 2) * bit
        bit *= 2
    return out


def kernel(dims, has_bias, *refs):
    n_coarse, n_fine, tokens, width, dec_rows = dims
    n_seq = n_coarse * n_fine
    n_q = n_fine // LOW
    n_kv = n_coarse * LOW
    n_pair_seq = n_seq // LOW
    half = n_fine // 2
    heads = width // HEAD
    pairs = heads // 2
    share = n_fine // pairs
    wide = width // LOW
    pairs_half = pairs // LOW
    refs = list(refs)
    ql, kl, vl, qh, kh, vh, enc, decq = refs[:8]
    bias_ref = refs[8] if has_bias else None
    (out, dec, encbuf, drows, dq, do, qbuf, kbuf, vbuf, acc, stat, osend, orecv,
     lq, lk, lv, lown, lsend, lrecv, band,
     load_s, enc_s, enc_r, ek_s, ek_r, q_s, q_r, k_s, k_r, v_s, v_r, kx_s, vx_s,
     x_s, x_r, h_s, h_r, o_s, o_r, lo_s, lo_r, dec_s, dec_r) = refs[8 + has_bias:]

    c = lax.axis_index("coarse")
    f = lax.axis_index("fine")
    here = c * n_fine + f
    me_q = lax.div(f, LOW)
    lo = lax.rem(f, LOW)
    me_kv = c * LOW + lo
    p = lax.div(f, share)
    s_me = lax.rem(f, share)
    hh = lax.div(f, half)
    g = lax.rem(f, half)
    two = lax.div(here, LOW)

    def remote(src, dst, ssem, rsem, device):
        return pltpu.make_async_remote_copy(
            src_ref=src, dst_ref=dst, send_sem=ssem, recv_sem=rsem,
            device_id=device, device_id_type=MESH,
        )

    def up(me, d, n):
        return lax.rem(me + d, n)

    def down(me, d, n):
        return lax.rem(me + n - d, n)

    def at(cc, ff):
        return {"coarse": cc, "fine": ff}

    def cols_of(pair):
        return pl.ds(pl.multiple_of(pair * PAIR, PAIR), PAIR)

    def side_of(which):
        return pl.ds(pl.multiple_of(which * wide, PAIR), wide)

    def loop(start, stop, body):
        def step(d, carry):
            body(d)
            return carry
        lax.fori_loop(start, stop, step, 0)

    loads = [
        pltpu.make_async_copy(enc, encbuf.at[me_kv, me_q], load_s.at[0]),
        pltpu.make_async_copy(kh.at[:, cols_of(p)], kbuf.at[c, f], load_s.at[1]),
        pltpu.make_async_copy(vh.at[:, cols_of(p)], vbuf.at[c, f], load_s.at[2]),
        pltpu.make_async_copy(qh.at[:, cols_of(p)], qbuf.at[p], load_s.at[3]),
        pltpu.make_async_copy(decq.at[c, g], drows, load_s.at[4]),
        pltpu.make_async_copy(kl.at[:, side_of(lo)], lk.at[1 + lo], load_s.at[5]),
        pltpu.make_async_copy(vl.at[:, side_of(lo)], lv.at[1 + lo], load_s.at[6]),
        pltpu.make_async_copy(ql.at[:, side_of(lo)], lq.at[lo], load_s.at[7]),
    ]
    for copy in loads:
        copy.start()

    barrier = pltpu.get_barrier_semaphore()

    def greet(d, carry):
        t = up(here, d, n_seq)
        pl.semaphore_signal(
            barrier, inc=1, device_id=at(lax.div(t, n_fine), lax.rem(t, n_fine)), device_id_type=MESH
        )
        return carry

    lax.fori_loop(1, n_seq, greet, 0)
    pl.semaphore_wait(barrier, n_seq - 1)

    def at_q(a):
        return at(c, a * LOW + lo)

    def at_kv(b):
        return at(lax.div(b, LOW), me_q * LOW + lax.rem(b, LOW))

    def enc_copy(d):
        return remote(enc, encbuf.at[me_kv, me_q], enc_s.at[d], enc_r.at[me_q], at_q(up(me_q, d, n_q)))

    def enc_arrival(d):
        src = down(me_q, d, n_q)
        return remote(enc, encbuf.at[me_kv, src], enc_s.at[d], enc_r.at[src], at_q(src))

    other = c * LOW + 1 - lo

    def enc_low():
        return remote(encbuf.at[me_kv], encbuf.at[me_kv], ek_s.at[0, 0], ek_r.at[me_kv], at_kv(other))

    def enc_far(d, relay):
        block = other if relay else me_kv
        peer = up(c, d, n_coarse) * LOW + lo
        return remote(encbuf.at[block], encbuf.at[block], ek_s.at[int(relay), d], ek_r.at[block], at_kv(peer))

    def enc_block(block):
        return remote(encbuf.at[block], encbuf.at[block], ek_s.at[0, 0], ek_r.at[block], at_kv(block))

    def q_copy(d):
        to = flip(p, d, pairs)
        return remote(qh.at[:, cols_of(to)], qbuf.at[p], q_s.at[d], q_r.at[p], at(c, to * share + s_me))

    def q_arrival(d):
        src = flip(p, d, pairs)
        return remote(qbuf.at[src], qbuf.at[src], q_s.at[d], q_r.at[src], at(c, src * share + s_me))

    def kv_copy(d):
        to = flip(f, d, n_fine)
        col = cols_of(lax.div(to, share))
        return (
            remote(kh.at[:, col], kbuf.at[c, f], k_s.at[d], k_r.at[c, f], at(c, to)),
            remote(vh.at[:, col], vbuf.at[c, f], v_s.at[d], v_r.at[c, f], at(c, to)),
        )

    def kv_block(cc, ff):
        return (
            remote(kbuf.at[cc, ff], kbuf.at[cc, ff], k_s.at[0], k_r.at[cc, ff], at(cc, ff)),
            remote(vbuf.at[cc, ff], vbuf.at[cc, ff], v_s.at[0], v_r.at[cc, ff], at(cc, ff)),
        )

    def kv_relay(d, e):
        src = flip(f, d, n_fine)
        peer = at(up(c, e, n_coarse), f)
        return (
            remote(kbuf.at[c, src], kbuf.at[c, src], kx_s.at[d, e], k_r.at[c, src], peer),
            remote(vbuf.at[c, src], vbuf.at[c, src], vx_s.at[d, e], v_r.at[c, src], peer),
        )

    def kv_forward(d):
        if d:
            for copy in kv_block(c, flip(f, d, n_fine)):
                copy.wait_recv()
        for e in range(1, n_coarse):
            for copy in kv_relay(d, e):
                copy.start()

    def o_copy(d):
        to = flip(p, d, pairs)
        return remote(osend.at[to], orecv.at[p], o_s.at[d], o_r.at[p], at(c, to * share + s_me))

    def o_arrival(d):
        src = flip(p, d, pairs)
        return remote(osend.at[src], orecv.at[src], o_s.at[d], o_r.at[src], at(c, src * share + s_me))

    mate = at(c, f + 1 - 2 * lo)

    def swap_copy():
        cols = side_of(1 - lo)
        return (
            remote(kl.at[:, cols], lk.at[1 + lo], x_s.at[0], x_r.at[0], mate),
            remote(vl.at[:, cols], lv.at[1 + lo], x_s.at[1], x_r.at[1], mate),
            remote(ql.at[:, cols], lq.at[lo], x_s.at[2], x_r.at[2], mate),
        )

    def swap_arrival():
        return (
            remote(lk.at[2 - lo], lk.at[2 - lo], x_s.at[0], x_r.at[0], mate),
            remote(lv.at[2 - lo], lv.at[2 - lo], x_s.at[1], x_r.at[1], mate),
            remote(lq.at[1 - lo], lq.at[1 - lo], x_s.at[2], x_r.at[2], mate),
        )

    def halo_copy(side):
        peer = jnp.clip(two + 2 * side - 1, 0, n_pair_seq - 1) * LOW + lo
        device = at(lax.div(peer, n_fine), lax.rem(peer, n_fine))
        slot = 3 - 3 * side
        return (
            remote(lk.at[1 + side], lk.at[slot], h_s.at[side, 0], h_r.at[side, 0], device),
            remote(lv.at[1 + side], lv.at[slot], h_s.at[side, 1], h_r.at[side, 1], device),
        )

    has_peer = [two > 0, two < n_pair_seq - 1]

    def light_back():
        return remote(lsend, lrecv, lo_s, lo_r, mate)

    bits = []
    bit = half // 2
    while bit:
        bits.append(bit)
        bit //= 2

    def dec_copy(block, k):
        mine = dec.at[c, block]
        if k < len(bits):
            peer = at(c, hh * half + flip(g, bits[k], half))
        else:
            peer = at(up(c, k - len(bits) + 1, n_coarse), f)
        return remote(mine, mine, dec_s.at[k, block], dec_r.at[c, block], peer)

    def dec_arrival(cc, block):
        part = dec.at[cc, block]
        return remote(part, part, dec_s.at[0, 0], dec_r.at[cc, block], at(cc, f))

    def dec_spread(block, first):
        for k in range(first, len(bits) + n_coarse - 1):
            dec_copy(block, k).start()

    def dec_stage(k):
        done = [0]
        for b in bits[:k]:
            done = done + [x + b for x in done]
        return [flip(g, x + bits[k], half) for x in done]

    def dec_forward(k):
        for block in dec_stage(k):
            dec_arrival(c, block).wait_recv()
            dec_spread(block, k + 1)

    for d in range(1, n_q):
        enc_copy(d).start()
    for d in [*range(pairs // 2, pairs), *range(1, pairs // 2)]:
        q_copy(d).start()
    loads[1].wait()
    loads[2].wait()
    kv_forward(0)

    row = lax.broadcasted_iota(jnp.int32, (tokens, 3 * tokens), 0)
    col = lax.broadcasted_iota(jnp.int32, (tokens, 3 * tokens), 1)
    for b in range(LOW):
        pos = (two * LOW + b) * tokens + col - tokens
        seen = (jnp.abs(col - tokens - row) <= ROUTED_BLOCK - 1) & (pos >= 0) & (pos < n_seq * tokens)
        band[b] = jnp.where(seen, jnp.float32(0), jnp.float32(NEG))

    loads[4].wait()
    lane_d = lax.broadcasted_iota(jnp.int32, (dec_rows, PAIR), 1)
    for j in range(pairs):
        q = drows[:, j * PAIR:(j + 1) * PAIR].astype(jnp.float32) * (HEAD ** (-0.5))
        swapped = pltpu.roll(q, HEAD, 1)
        both = jnp.concatenate(
            [jnp.where(lane_d < HEAD, q, 0.0), jnp.where(lane_d < HEAD, swapped, 0.0)], axis=0
        )
        dq[2 * j * dec_rows:(2 * j + 2) * dec_rows, :] = both.astype(jnp.bfloat16)

    loads[0].wait()
    for d in range(1, n_q):
        enc_arrival(d).wait_recv()
    enc_low().start()
    for d in range(1, n_coarse):
        enc_far(d, False).start()
    for d in range(1, n_fine):
        for copy in kv_copy(d):
            copy.start()
    loads[5].wait()
    loads[6].wait()

    for side in range(2):
        @pl.when((lo == side) & has_peer[side])
        def _():
            for copy in halo_copy(side):
                copy.start()

    enc_block(other).wait_recv()
    for d in range(1, n_coarse):
        enc_far(d, True).start()
    for copy in swap_copy():
        copy.start()

    for d in range(1, half):
        kv_forward(d)

    for d in range(1, n_coarse):
        for part in range(LOW):
            enc_block(up(c, d, n_coarse) * LOW + part).wait_recv()

    d_total = heads * dec_rows
    d_chunk = min(256, d_total)

    def dec_step(i):
        rows = pl.ds(pl.multiple_of(i * d_chunk, d_chunk), d_chunk)
        kv = encbuf[...].reshape(n_seq * tokens, PAIR)
        s = dot_t(dq[rows, :], kv)
        e = jnp.exp(s - jnp.max(s, axis=1, keepdims=True))
        total = jnp.sum(e, axis=1, keepdims=True)
        do[rows, :] = dot(e.astype(jnp.bfloat16), kv) / total

    loop(0, d_total // d_chunk, dec_step)
    for j in range(pairs):
        even = do[2 * j * dec_rows:(2 * j + 1) * dec_rows, :]
        odd = do[(2 * j + 1) * dec_rows:(2 * j + 2) * dec_rows, :]
        dec[c, g, :, j * PAIR:(j + 1) * PAIR] = jnp.where(
            lane_d < HEAD, pltpu.roll(even, HEAD, 1), odd
        ).astype(jnp.bfloat16)
    dec_spread(g, 0)

    low_half = lax.broadcasted_iota(jnp.int32, (tokens, PAIR), 1) < HEAD
    lane_2 = lax.broadcasted_iota(jnp.int32, (2 * tokens, PAIR), 1)
    keys = n_coarse * half * tokens

    def heavy_scores(j, part):
        q = stacked_pair(qbuf[j], low_half)
        s = dot_t(q, kbuf[:, pl.ds(part * half, half)].reshape(keys, PAIR))
        if has_bias:
            s = s + bias_ref[part, 0:1, :]
        return s

    def heavy_values(part):
        return vbuf[:, pl.ds(part * half, half)].reshape(keys, PAIR)

    def heavy_first(j):
        s = heavy_scores(j, hh)
        peak = jnp.max(s, axis=1, keepdims=True)
        e = jnp.exp(s - peak)
        total = jnp.sum(e, axis=1, keepdims=True)
        acc[j] = dot(e.astype(jnp.bfloat16), heavy_values(hh))
        stat[j] = jnp.where(lane_2 == 0, peak, total)

    def heavy_second(j):
        s = heavy_scores(j, 1 - hh)
        before = stat[j, :, 0:1]
        peak = jnp.maximum(before, jnp.max(s, axis=1, keepdims=True))
        e = jnp.exp(s - peak)
        keep = jnp.exp(before - peak)
        total = stat[j, :, 1:2] * keep + jnp.sum(e, axis=1, keepdims=True)
        o = (acc[j] * keep + dot(e.astype(jnp.bfloat16), heavy_values(1 - hh))) / total
        return jnp.where(low_half, o[:tokens], o[tokens:]).astype(jnp.bfloat16)

    loads[3].wait()
    for d in range(1, pairs):
        q_arrival(d).wait_recv()
    for e in range(1, n_coarse):
        for i in range(half):
            for copy in kv_block(up(c, e, n_coarse), hh * half + i):
                copy.wait_recv()
    per = max(1, pairs // half)
    done = 0
    for r in range(half):
        stop = pairs if r == half - 1 else min(pairs, done + per)
        loop(done, stop, heavy_first)
        done = stop
        kv_forward(half + r)

    for k in range(len(bits) - 1):
        dec_forward(k)
    arrived = swap_arrival()
    arrived[0].wait_recv()
    arrived[1].wait_recv()
    for side in range(2):
        @pl.when((lo == 1 - side) & has_peer[side])
        def _():
            for copy in halo_copy(side):
                copy.start()

    for e in range(1, n_coarse):
        for i in range(half):
            for copy in kv_block(up(c, e, n_coarse), (1 - hh) * half + i):
                copy.wait_recv()

    def heavy_out(i):
        d = pairs - 1 - i
        j = flip(p, d, pairs)
        osend[j] = heavy_second(j)
        o_copy(d).start()

    loop(0, pairs - 1, heavy_out)
    orecv[p] = heavy_second(p)
    dec_forward(len(bits) - 1)

    arrived[2].wait_recv()
    loads[7].wait()
    for side in range(2):
        @pl.when(has_peer[side])
        def _():
            for copy in halo_copy(1 - side):
                copy.wait_recv()

        @pl.when(jnp.logical_not(has_peer[side]))
        def _():
            lk[3 * side] = jnp.zeros((tokens, wide), jnp.bfloat16)
            lv[3 * side] = jnp.zeros((tokens, wide), jnp.bfloat16)

    def light_of(b, j):
        cols = cols_of(j)
        q = stacked_pair(lq[b, :, cols], low_half)
        mask = band[b]
        s = dot_t(q, lk[pl.ds(b, 3), :, cols].reshape(3 * tokens, PAIR))
        s = s + jnp.concatenate([mask, mask], axis=0)
        e = jnp.exp(s - jnp.max(s, axis=1, keepdims=True))
        total = jnp.sum(e, axis=1, keepdims=True)
        o = dot(e.astype(jnp.bfloat16), lv[pl.ds(b, 3), :, cols].reshape(3 * tokens, PAIR)) / total
        return jnp.where(low_half, o[:tokens], o[tokens:])

    def light_away(j):
        lsend[:, cols_of(j)] = light_of(1 - lo, j).astype(jnp.bfloat16)

    def light_home(j):
        lown[:, cols_of(j)] = light_of(lo, j)

    loop(0, pairs_half, light_away)
    light_back().start()
    loop(0, pairs_half, light_home)

    for d in range(1, pairs):
        o_arrival(d).wait_recv()

    def join_home(j):
        pair = lo * pairs_half + j
        heavy = orecv[pair].astype(jnp.float32)
        out[:, cols_of(pair)] = (lown[:, cols_of(j)] + heavy).astype(jnp.bfloat16)

    def join_away(j):
        pair = (1 - lo) * pairs_half + j
        heavy = orecv[pair].astype(jnp.float32)
        out[:, cols_of(pair)] = (lrecv[:, cols_of(j)].astype(jnp.float32) + heavy).astype(jnp.bfloat16)

    loop(0, pairs_half, join_home)
    light_back().wait_recv()
    loop(0, pairs_half, join_away)

    for e in range(1, n_coarse):
        for block in range(half):
            dec_arrival(up(c, e, n_coarse), block).wait_recv()
    for d in range(1, n_q):
        enc_copy(d).wait_send()
    enc_low().wait_send()
    for d in range(1, n_coarse):
        enc_far(d, False).wait_send()
        enc_far(d, True).wait_send()
    for d in range(1, pairs):
        q_copy(d).wait_send()
        o_copy(d).wait_send()
    for d in range(n_fine):
        if d:
            for copy in kv_copy(d):
                copy.wait_send()
        for e in range(1, n_coarse):
            for copy in kv_relay(d, e):
                copy.wait_send()
    for copy in swap_copy():
        copy.wait_send()
    light_back().wait_send()
    for side in range(2):
        @pl.when(has_peer[side])
        def _():
            for copy in halo_copy(side):
                copy.wait_send()
    for k in range(len(bits) + n_coarse - 1):
        sent = [0]
        for b in bits[:k]:
            sent = sent + [x + b for x in sent]
        for x in sent:
            dec_copy(flip(g, x, half), k).wait_send()


def local(
    q_light, k_light, v_light, q_heavy, k_heavy, v_heavy, enc_kv, dec_queries, query_ids, key_ids
):
    _, tokens, width = q_light.shape
    n_coarse = lax.axis_size("coarse")
    n_fine = lax.axis_size("fine")
    n_seq = n_coarse * n_fine
    n_q = n_fine // LOW
    n_kv = n_coarse * LOW
    half = n_fine // 2
    heads = width // HEAD
    pairs = heads // 2
    count = dec_queries.shape[1]
    dec_rows = count // (n_coarse * half)
    n_bits = half.bit_length() - 1
    mine = dec_queries.reshape(n_coarse, half, dec_rows, width)
    args = [q_light[0], k_light[0], v_light[0], q_heavy[0], k_heavy[0], v_heavy[0], enc_kv[0], mine]
    args = [pltpu.with_memory_space_constraint(a, pltpu.HBM) for a in args]
    has_bias = key_ids.shape[1] != n_seq
    keys = n_coarse * half * tokens
    if has_bias:
        blocks = jnp.arange(n_seq, dtype=jnp.int32).reshape(n_coarse, 2, half).transpose(1, 0, 2)
        listed = jnp.any(blocks[..., None] == key_ids[0], axis=-1).reshape(2, 1, n_coarse * half)
        bias = jnp.repeat(jnp.where(listed, 0.0, NEG).astype(jnp.float32), tokens, axis=2)
        args.append(jnp.broadcast_to(bias, (2, 8, keys)))
    bf16, f32 = jnp.bfloat16, jnp.float32
    dma = pltpu.SemaphoreType.DMA
    vmem = pl.BlockSpec(memory_space=pltpu.VMEM)
    hbm = pl.BlockSpec(memory_space=pltpu.HBM)
    wide = width // LOW
    encoded, decoded = pl.pallas_call(
        functools.partial(kernel, (n_coarse, n_fine, tokens, width, dec_rows), has_bias),
        out_shape=(
            jax.ShapeDtypeStruct((tokens, width), bf16),
            jax.ShapeDtypeStruct((n_coarse, half, dec_rows, width), bf16),
        ),
        in_specs=[hbm] * 8 + [vmem] * (len(args) - 8),
        out_specs=(vmem, vmem),
        scratch_shapes=[
            pltpu.VMEM((n_kv, n_q, tokens, PAIR), bf16),
            pltpu.VMEM((dec_rows, width), bf16),
            pltpu.VMEM((heads * dec_rows, PAIR), bf16),
            pltpu.VMEM((heads * dec_rows, PAIR), f32),
            pltpu.VMEM((pairs, tokens, PAIR), bf16),
            pltpu.VMEM((n_coarse, n_fine, tokens, PAIR), bf16),
            pltpu.VMEM((n_coarse, n_fine, tokens, PAIR), bf16),
            pltpu.VMEM((pairs, 2 * tokens, PAIR), f32),
            pltpu.VMEM((pairs, 2 * tokens, PAIR), f32),
            pltpu.VMEM((pairs, tokens, PAIR), bf16),
            pltpu.VMEM((pairs, tokens, PAIR), bf16),
            pltpu.VMEM((2, tokens, wide), bf16),
            pltpu.VMEM((4, tokens, wide), bf16),
            pltpu.VMEM((4, tokens, wide), bf16),
            pltpu.VMEM((tokens, wide), f32),
            pltpu.VMEM((tokens, wide), bf16),
            pltpu.VMEM((tokens, wide), bf16),
            pltpu.VMEM((2, tokens, 3 * tokens), f32),
            dma((8,)),
            dma((n_q,)), dma((n_q,)),
            dma((2, n_coarse)), dma((n_kv,)),
            dma((pairs,)), dma((pairs,)),
            dma((n_fine,)), dma((n_coarse, n_fine)),
            dma((n_fine,)), dma((n_coarse, n_fine)),
            dma((n_fine, n_coarse)), dma((n_fine, n_coarse)),
            dma((3,)), dma((3,)),
            dma((2, 2)), dma((2, 2)),
            dma((pairs,)), dma((pairs,)),
            dma, dma,
            dma((n_bits + n_coarse - 1, half)), dma((n_coarse, half)),
        ],
        compiler_params=pltpu.CompilerParams(
            collective_id=0, has_side_effects=True, vmem_limit_bytes=32 * 1024 * 1024
        ),
    )(*args)
    return encoded[None], decoded.reshape(1, count, width)


def solution(mesh):
    rows = P("doc", ("coarse", "fine"), None)
    placed = (rows,) * 7 + (P("doc", None, None), P("doc", None), P("doc", None))
    return jax.shard_map(
        local,
        mesh=mesh,
        in_specs=placed,
        out_specs=(rows, P("doc", None, None)),
        check_vma=False,
    )
```

```python
import functools

import jax
import jax.numpy as jnp
from jax import lax
from jax.experimental import pallas as pl
from jax.experimental.pallas import tpu as pltpu
from jax.sharding import PartitionSpec as P

HEAD = 64
PAIR = 2 * HEAD
ROUTED_BLOCK = 128
LOW = 2
MESH = pl.DeviceIdType.MESH
NEG = -1e30


def dot_t(a, b):
    return lax.dot_general(a, b, (((1,), (1,)), ((), ())), preferred_element_type=jnp.float32)


def dot(a, b):
    return jnp.dot(a, b, preferred_element_type=jnp.float32)


def stacked_pair(q, low_half):
    q = q * jnp.asarray(HEAD ** (-0.5), q.dtype)
    zero = jnp.zeros_like(q)
    return jnp.concatenate([jnp.where(low_half, q, zero), jnp.where(low_half, zero, q)], axis=0)


def flip(v, d, n):
    out, bit = 0, 1
    while bit < n:
        if isinstance(d, int):
            on = (d // bit) % 2
        else:
            on = lax.rem(lax.div(d, bit), 2)
        out = out + lax.rem(lax.div(v, bit) + on, 2) * bit
        bit *= 2
    return out


def kernel(dims, has_bias, *refs):
    n_coarse, n_fine, tokens, width, dec_rows = dims
    n_seq = n_coarse * n_fine
    n_q = n_fine // LOW
    n_kv = n_coarse * LOW
    n_pair_seq = n_seq // LOW
    half = n_fine // 2
    heads = width // HEAD
    pairs = heads // 2
    share = n_fine // pairs
    wide = width // LOW
    pairs_half = pairs // LOW
    refs = list(refs)
    ql, kl, vl, qh, kh, vh, enc, decq = refs[:8]
    bias_ref = refs[8] if has_bias else None
    (out, dec, encbuf, drows, dq, do, qbuf, kbuf, vbuf, acc, stat, osend, orecv,
     lq, lk, lv, hop, lown, lsend, lrecv, band,
     load_s, enc_s, enc_r, ey_s, ex_s, q_s, q_r, k_s, k_r, v_s, v_r, kx_s, vx_s,
     far_s, x_s, x_r, h_s, h_r, hop_s, hop_r, o_s, o_r, lo_s, lo_r, dec_s, dec_r) = refs[8 + has_bias:]

    c = lax.axis_index("coarse")
    f = lax.axis_index("fine")
    here = c * n_fine + f
    me_q = lax.div(f, LOW)
    lo = lax.rem(f, LOW)
    me_kv = c * LOW + lo
    p = lax.div(f, share)
    s_me = lax.rem(f, share)
    hh = lax.div(f, half)
    g = lax.rem(f, half)
    two = lax.div(here, LOW)

    def remote(src, dst, ssem, rsem, device):
        return pltpu.make_async_remote_copy(
            src_ref=src, dst_ref=dst, send_sem=ssem, recv_sem=rsem,
            device_id=device, device_id_type=MESH,
        )

    def up(me, d, n):
        return lax.rem(me + d, n)

    def down(me, d, n):
        return lax.rem(me + n - d, n)

    def at(cc, ff):
        return {"coarse": cc, "fine": ff}

    def cols_of(pair):
        return pl.ds(pl.multiple_of(pair * PAIR, PAIR), PAIR)

    def side_of(which):
        return pl.ds(pl.multiple_of(which * wide, PAIR), wide)

    def loop(start, stop, body):
        def step(d, carry):
            body(d)
            return carry
        lax.fori_loop(start, stop, step, 0)

    def begin(copies):
        for copy in copies:
            copy.start()

    def begin_if(cond, copies):
        @pl.when(cond)
        def _():
            begin(copies)

    loads = [
        pltpu.make_async_copy(enc, encbuf.at[me_kv, me_q], load_s.at[0]),
        pltpu.make_async_copy(kh.at[:, cols_of(p)], kbuf.at[c, f], load_s.at[1]),
        pltpu.make_async_copy(vh.at[:, cols_of(p)], vbuf.at[c, f], load_s.at[2]),
        pltpu.make_async_copy(qh.at[:, cols_of(p)], qbuf.at[p], load_s.at[3]),
        pltpu.make_async_copy(decq.at[c, g], drows, load_s.at[4]),
        pltpu.make_async_copy(kl.at[:, side_of(lo)], lk.at[1 + lo], load_s.at[5]),
        pltpu.make_async_copy(vl.at[:, side_of(lo)], lv.at[1 + lo], load_s.at[6]),
        pltpu.make_async_copy(ql.at[:, side_of(lo)], lq.at[lo], load_s.at[7]),
    ]
    for copy in loads:
        copy.start()

    barrier = pltpu.get_barrier_semaphore()

    has_up = me_q < n_q - 1
    has_down = me_q > 0
    n_near = n_coarse + has_up.astype(jnp.int32) + has_down.astype(jnp.int32)

    def greet(sem):
        def say(device):
            pl.semaphore_signal(sem, inc=1, device_id=device, device_id_type=MESH)

        say(at(c, f + 1 - 2 * lo))
        for e in range(1, n_coarse):
            say(at(up(c, e, n_coarse), f))

        @pl.when(has_up)
        def _():
            say(at(c, jnp.minimum(f + LOW, n_fine - 1)))

        @pl.when(has_down)
        def _():
            say(at(c, jnp.maximum(f - LOW, 0)))

    greet(barrier)
    pl.semaphore_wait(barrier, n_near)

    def round_out(r):
        greet(far_s.at[r])

    def round_in(r):
        pl.semaphore_wait(far_s.at[r], n_near)

    def enc_row(way):
        peer = jnp.clip(me_q + way, 0, n_q - 1)
        return remote(
            enc, encbuf.at[me_kv, me_q], enc_s.at[way + n_q - 1], enc_r.at[me_kv, me_q], at(c, peer * LOW + lo)
        )

    def enc_mate(block):
        part = encbuf.at[me_kv, block]
        return remote(part, part, ey_s.at[block], enc_r.at[me_kv, block], at(c, f + 1 - 2 * lo))

    def enc_across(low, block, e):
        part = encbuf.at[c * LOW + low, block]
        return remote(
            part, part, ex_s.at[low, e, block], enc_r.at[c * LOW + low, block], at(up(c, e, n_coarse), f)
        )

    def enc_wait(kv, block):
        part = encbuf.at[kv, block]
        remote(part, part, ey_s.at[block], enc_r.at[kv, block], at(c, f)).wait_recv()

    def enc_out(block):
        enc_mate(block).start()
        for e in range(1, n_coarse):
            enc_across(lo, block, e).start()

    def enc_at(t):
        for way in (t, -t):
            row = me_q + way
            yield way, jnp.clip(row, 0, n_q - 1), (row >= 0) & (row < n_q)

    def enc_rows(t):
        for way, row, there in enc_at(t):
            begin_if(there, (enc_row(way),))

    def enc_step(t):
        for way, row, there in enc_at(t):
            @pl.when(there)
            def _():
                enc_wait(me_kv, row)
                enc_out(row)

    def enc_turn(block):
        enc_wait(c * LOW + 1 - lo, block)
        for e in range(1, n_coarse):
            enc_across(1 - lo, block, e).start()

    def enc_side(t):
        for way, row, there in enc_at(t):
            @pl.when(there)
            def _():
                enc_turn(row)

    def q_copy(d):
        to = flip(p, d, pairs)
        return remote(qh.at[:, cols_of(to)], qbuf.at[p], q_s.at[d], q_r.at[p], at(c, to * share + s_me))

    def q_arrival(d):
        src = flip(p, d, pairs)
        return remote(qbuf.at[src], qbuf.at[src], q_s.at[d], q_r.at[src], at(c, src * share + s_me))

    def kv_copy(d):
        to = flip(f, d, n_fine)
        col = cols_of(lax.div(to, share))
        return (
            remote(kh.at[:, col], kbuf.at[c, f], k_s.at[d], k_r.at[c, f], at(c, to)),
            remote(vh.at[:, col], vbuf.at[c, f], v_s.at[d], v_r.at[c, f], at(c, to)),
        )

    def kv_block(cc, ff):
        return (
            remote(kbuf.at[cc, ff], kbuf.at[cc, ff], k_s.at[0], k_r.at[cc, ff], at(cc, ff)),
            remote(vbuf.at[cc, ff], vbuf.at[cc, ff], v_s.at[0], v_r.at[cc, ff], at(cc, ff)),
        )

    def kv_relay(d, e):
        src = flip(f, d, n_fine)
        peer = at(up(c, e, n_coarse), f)
        return (
            remote(kbuf.at[c, src], kbuf.at[c, src], kx_s.at[d, e], k_r.at[c, src], peer),
            remote(vbuf.at[c, src], vbuf.at[c, src], vx_s.at[d, e], v_r.at[c, src], peer),
        )

    def kv_forward(d):
        if d:
            for copy in kv_block(c, flip(f, d, n_fine)):
                copy.wait_recv()
        for e in range(1, n_coarse):
            for copy in kv_relay(d, e):
                copy.start()

    def o_copy(d):
        to = flip(p, d, pairs)
        return remote(osend.at[to], orecv.at[p], o_s.at[d], o_r.at[p], at(c, to * share + s_me))

    def o_arrival(d):
        src = flip(p, d, pairs)
        return remote(osend.at[src], orecv.at[src], o_s.at[d], o_r.at[src], at(c, src * share + s_me))

    mate = at(c, f + 1 - 2 * lo)

    def swap_copy():
        cols = side_of(1 - lo)
        return (
            remote(kl.at[:, cols], lk.at[1 + lo], x_s.at[0], x_r.at[0], mate),
            remote(vl.at[:, cols], lv.at[1 + lo], x_s.at[1], x_r.at[1], mate),
            remote(ql.at[:, cols], lq.at[lo], x_s.at[2], x_r.at[2], mate),
        )

    def swap_arrival():
        return (
            remote(lk.at[2 - lo], lk.at[2 - lo], x_s.at[0], x_r.at[0], mate),
            remote(lv.at[2 - lo], lv.at[2 - lo], x_s.at[1], x_r.at[1], mate),
            remote(lq.at[1 - lo], lq.at[1 - lo], x_s.at[2], x_r.at[2], mate),
        )

    def halo_copy(side):
        peer = jnp.clip(two + 2 * side - 1, 0, n_pair_seq - 1) * LOW + lo
        device = at(lax.div(peer, n_fine), lax.rem(peer, n_fine))
        slot = 3 - 3 * side
        return (
            remote(lk.at[1 + side], lk.at[slot], h_s.at[side, 0], h_r.at[side, 0], device),
            remote(lv.at[1 + side], lv.at[slot], h_s.at[side, 1], h_r.at[side, 1], device),
        )

    has_peer = [two > 0, two < n_pair_seq - 1]
    at_edge = [me_q == 0, me_q == n_q - 1]

    def hop_copy(side):
        peer = jnp.clip(c + 2 * side - 1, 0, n_coarse - 1)
        return remote(lv.at[1 + side], hop, h_s.at[side, 1], hop_r, at(peer, f))

    def hop_on(side):
        end = (1 - side) * (n_q - 1)
        slot = 3 - 3 * side
        return remote(hop, lv.at[slot], hop_s, h_r.at[side, 1], at(c, end * LOW + lo))

    hops_here = [at_edge[0] & (c < n_coarse - 1), at_edge[1] & (c > 0)]

    def halo_send(side, mine):
        go = mine & has_peer[side]
        keys, values = halo_copy(side)

        @pl.when(go)
        def _():
            keys.start()

        @pl.when(go & jnp.logical_not(at_edge[side]))
        def _():
            values.start()

        @pl.when(go & at_edge[side])
        def _():
            hop_copy(side).start()

    def hop_forward():
        for side in range(2):
            @pl.when(hops_here[side])
            def _():
                hop_copy(side).wait_recv()
                hop_on(side).start()

    def light_back(j):
        return remote(lsend.at[j], lrecv.at[j], lo_s.at[j], lo_r.at[j], mate)

    bits = []
    bit = half // 2
    while bit:
        bits.append(bit)
        bit //= 2

    def dec_copy(block, k):
        mine = dec.at[c, block]
        if k < len(bits):
            peer = at(c, hh * half + flip(g, bits[k], half))
        else:
            peer = at(up(c, k - len(bits) + 1, n_coarse), f)
        return remote(mine, mine, dec_s.at[k, block], dec_r.at[c, block], peer)

    def dec_arrival(cc, block):
        part = dec.at[cc, block]
        return remote(part, part, dec_s.at[0, 0], dec_r.at[cc, block], at(cc, f))

    def dec_spread(block, first):
        for k in range(first, len(bits)):
            dec_copy(block, k).start()

    def dec_across(block):
        for k in range(len(bits), len(bits) + n_coarse - 1):
            dec_copy(block, k).start()

    def dec_wave(steps):
        for x in range(1, half):
            if bin(x).count("1") == steps:
                block = flip(g, x, half)
                last = bits.index(x & -x)
                dec_arrival(c, block).wait_recv()
                dec_spread(block, last + 1)
                dec_across(block)

    def q_of(d):
        return (q_copy(d // share),) if d % share == 0 else ()

    def rows_next(d):
        return jnp.abs(lax.div(flip(f, d, n_fine), LOW) - me_q) == 1

    even_near, even_far = range(2, half, 2), range(half, n_fine, 2)
    odd_near, odd_far = range(3, half, 2), range(half + 1, n_fine, 2)
    even = [*even_near, *even_far]

    round_out(1)
    enc_rows(1)
    loads[0].wait()
    enc_out(me_q)
    for d in even:
        begin_if(rows_next(d), q_of(d))
    begin(q_of(1))
    loads[1].wait()
    loads[2].wait()
    kv_forward(0)
    for d in even:
        begin_if(rows_next(d), kv_copy(d))
    begin(kv_copy(1))
    row = lax.broadcasted_iota(jnp.int32, (tokens, 3 * tokens), 0)
    col = lax.broadcasted_iota(jnp.int32, (tokens, 3 * tokens), 1)
    for b in range(LOW):
        pos = (two * LOW + b) * tokens + col - tokens
        seen = (jnp.abs(col - tokens - row) <= ROUTED_BLOCK - 1) & (pos >= 0) & (pos < n_seq * tokens)
        band[b] = jnp.where(seen, jnp.float32(0), jnp.float32(NEG))

    loads[4].wait()
    lane_d = lax.broadcasted_iota(jnp.int32, (dec_rows, PAIR), 1)
    for j in range(pairs):
        q = drows[:, j * PAIR:(j + 1) * PAIR].astype(jnp.float32) * (HEAD ** (-0.5))
        swapped = pltpu.roll(q, HEAD, 1)
        both = jnp.concatenate(
            [jnp.where(lane_d < HEAD, q, 0.0), jnp.where(lane_d < HEAD, swapped, 0.0)], axis=0
        )
        dq[2 * j * dec_rows:(2 * j + 2) * dec_rows, :] = both.astype(jnp.bfloat16)

    for r in range(1, n_q - 1):
        round_in(r)
        round_out(r + 1)
    enc_step(1)
    round_in(n_q - 1)
    for t in range(2, n_q):
        enc_rows(t)
    for d in [*odd_near, *even]:
        begin_if(jnp.logical_not(rows_next(d)) if d % 2 == 0 else here >= 0, q_of(d))
    for d in odd_far:
        begin(q_of(d))
    for d in odd_near:
        begin(kv_copy(d))
    enc_turn(me_q)
    enc_side(1)
    for d in even:
        begin_if(jnp.logical_not(rows_next(d)), kv_copy(d))
    for d in range(2, half, 2):
        kv_forward(d)
    for d in range(1, half, 2):
        kv_forward(d)
    for t in range(2, n_q):
        enc_step(t)
    for d in odd_far:
        begin(kv_copy(d))
    begin(swap_copy())
    far = [*range(half, n_fine, 2), *range(half + 1, n_fine, 2)]
    quarter = len(far) // 4
    d_total = heads * dec_rows
    d_chunk = min(256, d_total)

    def dec_step(i):
        rows = pl.ds(pl.multiple_of(i * d_chunk, d_chunk), d_chunk)
        kv = encbuf[...].reshape(n_seq * tokens, PAIR)
        s = dot_t(dq[rows, :], kv)
        e = jnp.exp(s - jnp.max(s, axis=1, keepdims=True))
        total = jnp.sum(e, axis=1, keepdims=True)
        do[rows, :] = dot(e.astype(jnp.bfloat16), kv) / total

    low_half = lax.broadcasted_iota(jnp.int32, (tokens, PAIR), 1) < HEAD
    lane_2 = lax.broadcasted_iota(jnp.int32, (2 * tokens, PAIR), 1)
    keys = n_coarse * half * tokens

    def heavy_scores(j, part):
        q = stacked_pair(qbuf[j], low_half)
        s = dot_t(q, kbuf[:, pl.ds(part * half, half)].reshape(keys, PAIR))
        if has_bias:
            s = s + bias_ref[part, 0:1, :]
        return s

    def heavy_values(part):
        return vbuf[:, pl.ds(part * half, half)].reshape(keys, PAIR)

    def heavy_first(d):
        j = flip(p, d, pairs)
        s = heavy_scores(j, hh)
        peak = jnp.max(s, axis=1, keepdims=True)
        e = jnp.exp(s - peak)
        total = jnp.sum(e, axis=1, keepdims=True)
        acc[j] = dot(e.astype(jnp.bfloat16), heavy_values(hh))
        stat[j] = jnp.where(lane_2 == 0, peak, total)

    def heavy_second(j):
        s = heavy_scores(j, 1 - hh)
        before = stat[j, :, 0:1]
        peak = jnp.maximum(before, jnp.max(s, axis=1, keepdims=True))
        e = jnp.exp(s - peak)
        keep = jnp.exp(before - peak)
        total = stat[j, :, 1:2] * keep + jnp.sum(e, axis=1, keepdims=True)
        o = (acc[j] * keep + dot(e.astype(jnp.bfloat16), heavy_values(1 - hh))) / total
        return jnp.where(low_half, o[:tokens], o[tokens:]).astype(jnp.bfloat16)

    loads[3].wait()
    for d in range(1, pairs // 2):
        q_arrival(d).wait_recv()
    for e in range(1, n_coarse):
        for i in range(half):
            for copy in kv_block(up(c, e, n_coarse), hh * half + i):
                copy.wait_recv()
    loop(0, pairs // 2, heavy_first)
    for t in range(2, n_q):
        enc_side(t)
    arrived = swap_arrival()
    n_chunk = d_total // d_chunk
    for d in range(pairs // 2, pairs):
        q_arrival(d).wait_recv()
    loop(pairs // 2, pairs, heavy_first)
    for d in far[0 * quarter:1 * quarter]:
        kv_forward(d)
    for d in range(1, n_coarse):
        for part in range(LOW):
            for block in range(n_q):
                enc_wait(up(c, d, n_coarse) * LOW + part, block)

    loop(0 * n_chunk // 4, 1 * n_chunk // 4, dec_step)
    for d in far[1 * quarter:2 * quarter]:
        kv_forward(d)
    loop(1 * n_chunk // 4, 2 * n_chunk // 4, dec_step)
    for d in far[2 * quarter:3 * quarter]:
        kv_forward(d)
    loads[5].wait()
    loads[6].wait()
    for side in range(2):
        halo_send(side, lo == side)
    loop(2 * n_chunk // 4, 3 * n_chunk // 4, dec_step)
    for d in far[3 * quarter:4 * quarter]:
        kv_forward(d)
    loop(3 * n_chunk // 4, n_chunk, dec_step)
    for j in range(pairs):
        even = do[2 * j * dec_rows:(2 * j + 1) * dec_rows, :]
        odd = do[(2 * j + 1) * dec_rows:(2 * j + 2) * dec_rows, :]
        dec[c, g, :, j * PAIR:(j + 1) * PAIR] = jnp.where(
            lane_d < HEAD, pltpu.roll(even, HEAD, 1), odd
        ).astype(jnp.bfloat16)
    dec_spread(g, 0)
    arrived[0].wait_recv()
    arrived[1].wait_recv()
    for side in range(2):
        halo_send(side, lo == 1 - side)
    hop_forward()
    dec_across(g)
    for e in range(1, n_coarse):
        for i in range(half):
            for copy in kv_block(up(c, e, n_coarse), (1 - hh) * half + i):
                copy.wait_recv()

    def heavy_out(i):
        d = pairs - 1 - i
        j = flip(p, d, pairs)
        osend[j] = heavy_second(j)
        o_copy(d).start()

    loop(0, pairs // 2, heavy_out)
    dec_wave(1)
    loop(pairs // 2, pairs - 1, heavy_out)
    orecv[p] = heavy_second(p)

    arrived[2].wait_recv()
    loads[7].wait()
    for side in range(2):
        @pl.when(has_peer[side])
        def _():
            for copy in halo_copy(1 - side):
                copy.wait_recv()

        @pl.when(jnp.logical_not(has_peer[side]))
        def _():
            lk[3 * side] = jnp.zeros((tokens, wide), jnp.bfloat16)
            lv[3 * side] = jnp.zeros((tokens, wide), jnp.bfloat16)

    def light_of(b, j):
        cols = cols_of(j)
        q = stacked_pair(lq[b, :, cols], low_half)
        mask = band[b]
        s = dot_t(q, lk[pl.ds(b, 3), :, cols].reshape(3 * tokens, PAIR))
        s = s + jnp.concatenate([mask, mask], axis=0)
        e = jnp.exp(s - jnp.max(s, axis=1, keepdims=True))
        total = jnp.sum(e, axis=1, keepdims=True)
        o = dot(e.astype(jnp.bfloat16), lv[pl.ds(b, 3), :, cols].reshape(3 * tokens, PAIR)) / total
        return jnp.where(low_half, o[:tokens], o[tokens:])

    def light_away(j):
        lsend[j] = light_of(1 - lo, j).astype(jnp.bfloat16)
        light_back(j).start()

    def light_home(j):
        lown[:, cols_of(j)] = light_of(lo, j)

    loop(0, pairs_half, light_away)
    for steps in range(2, len(bits) + 1):
        dec_wave(steps)
    loop(0, pairs_half, light_home)

    for d in range(1, pairs):
        o_arrival(d).wait_recv()

    def join_home(j):
        pair = lo * pairs_half + j
        heavy = orecv[pair].astype(jnp.float32)
        out[:, cols_of(pair)] = (lown[:, cols_of(j)] + heavy).astype(jnp.bfloat16)

    def join_away(j):
        pair = (1 - lo) * pairs_half + j
        heavy = orecv[pair].astype(jnp.float32)
        out[:, cols_of(pair)] = (lrecv[j].astype(jnp.float32) + heavy).astype(jnp.bfloat16)

    loop(0, pairs_half, join_home)
    for j in range(pairs_half):
        light_back(j).wait_recv()
    loop(0, pairs_half, join_away)

    for e in range(1, n_coarse):
        for block in range(half):
            dec_arrival(up(c, e, n_coarse), block).wait_recv()
    for t in range(1, n_q):
        for way, row, there in enc_at(t):
            @pl.when(there)
            def _():
                enc_row(way).wait_send()

    for block in range(n_q):
        enc_mate(block).wait_send()
        for low in range(LOW):
            for e in range(1, n_coarse):
                enc_across(low, block, e).wait_send()
    for d in range(1, pairs):
        q_copy(d).wait_send()
        o_copy(d).wait_send()
    for d in range(n_fine):
        if d:
            for copy in kv_copy(d):
                copy.wait_send()
        for e in range(1, n_coarse):
            for copy in kv_relay(d, e):
                copy.wait_send()
    for copy in swap_copy():
        copy.wait_send()
    for j in range(pairs_half):
        light_back(j).wait_send()
    for side in range(2):
        @pl.when(has_peer[side])
        def _():
            for copy in halo_copy(side):
                copy.wait_send()

        @pl.when(hops_here[side])
        def _():
            hop_on(side).wait_send()
    for k in range(len(bits) + n_coarse - 1):
        sent = [0]
        for b in bits[:k]:
            sent = sent + [x + b for x in sent]
        for x in sent:
            dec_copy(flip(g, x, half), k).wait_send()


def local(
    q_light, k_light, v_light, q_heavy, k_heavy, v_heavy, enc_kv, dec_queries, query_ids, key_ids
):
    _, tokens, width = q_light.shape
    n_coarse = lax.axis_size("coarse")
    n_fine = lax.axis_size("fine")
    n_seq = n_coarse * n_fine
    n_q = n_fine // LOW
    n_kv = n_coarse * LOW
    half = n_fine // 2
    heads = width // HEAD
    pairs = heads // 2
    count = dec_queries.shape[1]
    dec_rows = count // (n_coarse * half)
    n_bits = half.bit_length() - 1
    mine = dec_queries.reshape(n_coarse, half, dec_rows, width)
    args = [q_light[0], k_light[0], v_light[0], q_heavy[0], k_heavy[0], v_heavy[0], enc_kv[0], mine]
    args = [pltpu.with_memory_space_constraint(a, pltpu.HBM) for a in args]
    has_bias = key_ids.shape[1] != n_seq
    keys = n_coarse * half * tokens
    if has_bias:
        blocks = jnp.arange(n_seq, dtype=jnp.int32).reshape(n_coarse, 2, half).transpose(1, 0, 2)
        listed = jnp.any(blocks[..., None] == key_ids[0], axis=-1).reshape(2, 1, n_coarse * half)
        bias = jnp.repeat(jnp.where(listed, 0.0, NEG).astype(jnp.float32), tokens, axis=2)
        args.append(jnp.broadcast_to(bias, (2, 8, keys)))
    bf16, f32 = jnp.bfloat16, jnp.float32
    dma = pltpu.SemaphoreType.DMA
    vmem = pl.BlockSpec(memory_space=pltpu.VMEM)
    hbm = pl.BlockSpec(memory_space=pltpu.HBM)
    wide = width // LOW
    encoded, decoded = pl.pallas_call(
        functools.partial(kernel, (n_coarse, n_fine, tokens, width, dec_rows), has_bias),
        out_shape=(
            jax.ShapeDtypeStruct((tokens, width), bf16),
            jax.ShapeDtypeStruct((n_coarse, half, dec_rows, width), bf16),
        ),
        in_specs=[hbm] * 8 + [vmem] * (len(args) - 8),
        out_specs=(vmem, vmem),
        scratch_shapes=[
            pltpu.VMEM((n_kv, n_q, tokens, PAIR), bf16),
            pltpu.VMEM((dec_rows, width), bf16),
            pltpu.VMEM((heads * dec_rows, PAIR), bf16),
            pltpu.VMEM((heads * dec_rows, PAIR), f32),
            pltpu.VMEM((pairs, tokens, PAIR), bf16),
            pltpu.VMEM((n_coarse, n_fine, tokens, PAIR), bf16),
            pltpu.VMEM((n_coarse, n_fine, tokens, PAIR), bf16),
            pltpu.VMEM((pairs, 2 * tokens, PAIR), f32),
            pltpu.VMEM((pairs, 2 * tokens, PAIR), f32),
            pltpu.VMEM((pairs, tokens, PAIR), bf16),
            pltpu.VMEM((pairs, tokens, PAIR), bf16),
            pltpu.VMEM((2, tokens, wide), bf16),
            pltpu.VMEM((4, tokens, wide), bf16),
            pltpu.VMEM((4, tokens, wide), bf16),
            pltpu.VMEM((tokens, wide), bf16),
            pltpu.VMEM((tokens, wide), f32),
            pltpu.VMEM((pairs // LOW, tokens, PAIR), bf16),
            pltpu.VMEM((pairs // LOW, tokens, PAIR), bf16),
            pltpu.VMEM((2, tokens, 3 * tokens), f32),
            dma((8,)),
            dma((2 * n_q - 1,)), dma((n_kv, n_q)),
            dma((n_q,)), dma((LOW, n_coarse, n_q)),
            dma((pairs,)), dma((pairs,)),
            dma((n_fine,)), dma((n_coarse, n_fine)),
            dma((n_fine,)), dma((n_coarse, n_fine)),
            dma((n_fine, n_coarse)), dma((n_fine, n_coarse)),
            pltpu.SemaphoreType.REGULAR((n_q,)),
            dma((3,)), dma((3,)),
            dma((2, 2)), dma((2, 2)),
            dma, dma,
            dma((pairs,)), dma((pairs,)),
            dma((pairs // LOW,)), dma((pairs // LOW,)),
            dma((n_bits + n_coarse - 1, half)), dma((n_coarse, half)),
        ],
        compiler_params=pltpu.CompilerParams(
            collective_id=0, has_side_effects=True, vmem_limit_bytes=32 * 1024 * 1024
        ),
    )(*args)
    return encoded[None], decoded.reshape(1, count, width)


def solution(mesh):
    rows = P("doc", ("coarse", "fine"), None)
    placed = (rows,) * 7 + (P("doc", None, None), P("doc", None), P("doc", None))
    return jax.shard_map(
        local,
        mesh=mesh,
        in_specs=placed,
        out_specs=(rows, P("doc", None, None)),
        check_vma=False,
    )
```

```python
import functools

import jax
import jax.numpy as jnp
from jax import lax
from jax.experimental import pallas as pl
from jax.experimental.pallas import tpu as pltpu
from jax.sharding import PartitionSpec as P

HEAD = 64
PAIR = 2 * HEAD
ROUTED_BLOCK = 128
LOW = 2
MESH = pl.DeviceIdType.MESH
NEG = -1e30


def dot_t(a, b):
    return lax.dot_general(a, b, (((1,), (1,)), ((), ())), preferred_element_type=jnp.float32)


def dot(a, b):
    return jnp.dot(a, b, preferred_element_type=jnp.float32)


def stacked_pair(q, low_half):
    q = q * jnp.asarray(HEAD ** (-0.5), q.dtype)
    zero = jnp.zeros_like(q)
    return jnp.concatenate([jnp.where(low_half, q, zero), jnp.where(low_half, zero, q)], axis=0)


def flip(v, d, n):
    out, bit = 0, 1
    while bit < n:
        if isinstance(d, int):
            on = (d // bit) % 2
        else:
            on = lax.rem(lax.div(d, bit), 2)
        out = out + lax.rem(lax.div(v, bit) + on, 2) * bit
        bit *= 2
    return out


def kernel(dims, has_bias, *refs):
    n_coarse, n_fine, tokens, width, dec_rows = dims
    n_seq = n_coarse * n_fine
    n_q = n_fine // LOW
    n_kv = n_coarse * LOW
    n_pair_seq = n_seq // LOW
    half = n_fine // 2
    heads = width // HEAD
    pairs = heads // 2
    share = n_fine // pairs
    wide = width // LOW
    pairs_half = pairs // LOW
    refs = list(refs)
    ql, kl, vl, qh, kh, vh, enc, decq = refs[:8]
    bias_ref = refs[8] if has_bias else None
    (out, dec, encbuf, drows, dq, do, qbuf, kvbuf, acc, stat, osend, orecv,
     lq, lk, lv, hop, lown, lsend, lrecv, band,
     load_s, enc_s, enc_r, ey_s, ex_s, q_s, q_r, kv_s, kv_r, kx_s,
     far_s, x_s, x_r, h_s, h_r, hop_s, hop_r, o_s, o_r, lo_s, lo_r, dec_s, dec_r) = refs[8 + has_bias:]

    c = lax.axis_index("coarse")
    f = lax.axis_index("fine")
    here = c * n_fine + f
    me_q = lax.div(f, LOW)
    lo = lax.rem(f, LOW)
    me_kv = c * LOW + lo
    p = lax.div(f, share)
    s_me = lax.rem(f, share)
    hh = lax.div(f, half)
    g = lax.rem(f, half)
    two = lax.div(here, LOW)

    def remote(src, dst, ssem, rsem, device):
        return pltpu.make_async_remote_copy(
            src_ref=src, dst_ref=dst, send_sem=ssem, recv_sem=rsem,
            device_id=device, device_id_type=MESH,
        )

    def take(ref, sem):
        remote(ref, ref, sem, sem, at(c, f)).wait_recv()

    def drain(ref, sem):
        remote(ref, ref, sem, sem, at(c, f)).wait_send()

    def up(me, d, n):
        return lax.rem(me + d, n)

    def down(me, d, n):
        return lax.rem(me + n - d, n)

    def at(cc, ff):
        return {"coarse": cc, "fine": ff}

    def cols_of(pair):
        return pl.ds(pl.multiple_of(pair * PAIR, PAIR), PAIR)

    def side_of(which):
        return pl.ds(pl.multiple_of(which * wide, PAIR), wide)

    def loop(start, stop, body):
        def step(d, carry):
            body(d)
            return carry
        lax.fori_loop(start, stop, step, 0)

    def begin(copies):
        for copy in copies:
            copy.start()

    def begin_if(cond, copies):
        @pl.when(cond)
        def _():
            begin(copies)

    loads = [
        pltpu.make_async_copy(enc, encbuf.at[me_kv, me_q], load_s.at[0]),
        pltpu.make_async_copy(kh.at[:, cols_of(p)], kvbuf.at[c, f, 0], load_s.at[1]),
        pltpu.make_async_copy(vh.at[:, cols_of(p)], kvbuf.at[c, f, 1], load_s.at[1]),
        pltpu.make_async_copy(qh.at[:, cols_of(p)], qbuf.at[p], load_s.at[2]),
        pltpu.make_async_copy(decq.at[c, g], drows, load_s.at[3]),
        pltpu.make_async_copy(kl.at[:, side_of(lo)], lk.at[1 + lo], load_s.at[4]),
        pltpu.make_async_copy(vl.at[:, side_of(lo)], lv.at[1 + lo], load_s.at[4]),
        pltpu.make_async_copy(ql.at[:, side_of(lo)], lq.at[lo], load_s.at[5]),
    ]
    for copy in loads:
        copy.start()

    barrier = pltpu.get_barrier_semaphore()

    has_up = me_q < n_q - 1
    has_down = me_q > 0
    n_near = n_coarse + has_up.astype(jnp.int32) + has_down.astype(jnp.int32)

    def greet(sem):
        def say(device):
            pl.semaphore_signal(sem, inc=1, device_id=device, device_id_type=MESH)

        say(at(c, f + 1 - 2 * lo))
        for e in range(1, n_coarse):
            say(at(up(c, e, n_coarse), f))

        @pl.when(has_up)
        def _():
            say(at(c, jnp.minimum(f + LOW, n_fine - 1)))

        @pl.when(has_down)
        def _():
            say(at(c, jnp.maximum(f - LOW, 0)))

    greet(barrier)
    pl.semaphore_wait(barrier, n_near)

    def round_out(r):
        greet(far_s.at[r])

    def round_in(r):
        pl.semaphore_wait(far_s.at[r], n_near)

    def enc_row(way):
        peer = jnp.clip(me_q + way, 0, n_q - 1)
        return remote(
            enc, encbuf.at[me_kv, me_q], enc_s, enc_r.at[me_q], at(c, peer * LOW + lo)
        )

    def enc_mate(block):
        part = encbuf.at[me_kv, block]
        return remote(part, part, ey_s, enc_r.at[n_q + block], at(c, f + 1 - 2 * lo))

    def enc_across(low, block, e):
        part = encbuf.at[c * LOW + low, block]
        return remote(part, part, ex_s, enc_r.at[2 * n_q], at(up(c, e, n_coarse), f))

    def enc_out(block):
        enc_mate(block).start()
        for e in range(1, n_coarse):
            enc_across(lo, block, e).start()

    def enc_at(t):
        for way in (t, -t):
            row = me_q + way
            yield way, jnp.clip(row, 0, n_q - 1), (row >= 0) & (row < n_q)

    def enc_rows(t):
        for way, row, there in enc_at(t):
            begin_if(there, (enc_row(way),))

    def enc_step(t):
        for way, row, there in enc_at(t):
            @pl.when(there)
            def _():
                take(encbuf.at[me_kv, row], enc_r.at[row])
                enc_out(row)

    def enc_turn(block):
        take(encbuf.at[c * LOW + 1 - lo, block], enc_r.at[n_q + block])
        for e in range(1, n_coarse):
            enc_across(1 - lo, block, e).start()

    def enc_side(t):
        for way, row, there in enc_at(t):
            @pl.when(there)
            def _():
                enc_turn(row)

    def q_copy(d):
        to = flip(p, d, pairs)
        return remote(qh.at[:, cols_of(to)], qbuf.at[p], q_s, q_r.at[int(d >= pairs // 2)], at(c, to * share + s_me))

    def kv_copy(d):
        to = flip(f, d, n_fine)
        col = cols_of(lax.div(to, share))
        return (
            remote(kh.at[:, col], kvbuf.at[c, f, 0], kv_s, kv_r.at[f], at(c, to)),
            remote(vh.at[:, col], kvbuf.at[c, f, 1], kv_s, kv_r.at[f], at(c, to)),
        )

    def kv_forward(d):
        src = flip(f, d, n_fine)
        block = kvbuf.at[c, src]
        if d:
            take(block, kv_r.at[src])
        for e in range(1, n_coarse):
            remote(block, block, kx_s, kv_r.at[n_fine + int(d >= half)], at(up(c, e, n_coarse), f)).start()

    def kv_others(far_half):
        take(kvbuf.at[pl.ds(0, n_coarse - 1), pl.ds(0, half)], kv_r.at[n_fine + far_half])

    def o_copy(d):
        to = flip(p, d, pairs)
        return remote(osend.at[to], orecv.at[p], o_s, o_r, at(c, to * share + s_me))

    mate = at(c, f + 1 - 2 * lo)

    def swap_copy():
        cols = side_of(1 - lo)
        return (
            remote(kl.at[:, cols], lk.at[1 + lo], x_s, x_r.at[0], mate),
            remote(vl.at[:, cols], lv.at[1 + lo], x_s, x_r.at[0], mate),
            remote(ql.at[:, cols], lq.at[lo], x_s, x_r.at[1], mate),
        )

    def halo_copy(side):
        peer = jnp.clip(two + 2 * side - 1, 0, n_pair_seq - 1) * LOW + lo
        device = at(lax.div(peer, n_fine), lax.rem(peer, n_fine))
        slot = 3 - 3 * side
        return (
            remote(lk.at[1 + side], lk.at[slot], h_s.at[side], h_r.at[side], device),
            remote(lv.at[1 + side], lv.at[slot], h_s.at[side], h_r.at[side], device),
        )

    has_peer = [two > 0, two < n_pair_seq - 1]
    at_edge = [me_q == 0, me_q == n_q - 1]

    def hop_copy(side):
        peer = jnp.clip(c + 2 * side - 1, 0, n_coarse - 1)
        return remote(lv.at[1 + side], hop, h_s.at[side], hop_r, at(peer, f))

    def hop_on(side):
        end = (1 - side) * (n_q - 1)
        slot = 3 - 3 * side
        return remote(hop, lv.at[slot], hop_s, h_r.at[side], at(c, end * LOW + lo))

    hops_here = [at_edge[0] & (c < n_coarse - 1), at_edge[1] & (c > 0)]

    def halo_send(side, mine):
        go = mine & has_peer[side]
        keys, values = halo_copy(side)

        @pl.when(go)
        def _():
            keys.start()

        @pl.when(go & jnp.logical_not(at_edge[side]))
        def _():
            values.start()

        @pl.when(go & at_edge[side])
        def _():
            hop_copy(side).start()

    def hop_forward():
        for side in range(2):
            @pl.when(hops_here[side])
            def _():
                hop_copy(side).wait_recv()
                hop_on(side).start()

    def light_back(j):
        return remote(lsend.at[j], lrecv.at[j], lo_s, lo_r, mate)

    bits = []
    bit = half // 2
    while bit:
        bits.append(bit)
        bit //= 2

    def dec_copy(block, k):
        mine = dec.at[c, block]
        if k < len(bits):
            peer = at(c, hh * half + flip(g, bits[k], half))
        else:
            peer = at(up(c, k - len(bits) + 1, n_coarse), f)
        return remote(mine, mine, dec_s.at[k], dec_r.at[block if k < len(bits) else half], peer)

    def dec_spread(block, first):
        for k in range(first, len(bits)):
            dec_copy(block, k).start()

    def dec_across(block):
        for k in range(len(bits), len(bits) + n_coarse - 1):
            dec_copy(block, k).start()

    def dec_wave(steps):
        for x in range(1, half):
            if bin(x).count("1") == steps:
                block = flip(g, x, half)
                last = bits.index(x & -x)
                take(dec.at[c, block], dec_r.at[block])
                dec_spread(block, last + 1)
                dec_across(block)

    def q_of(d):
        return (q_copy(d // share),) if d % share == 0 else ()

    def rows_next(d):
        return jnp.abs(lax.div(flip(f, d, n_fine), LOW) - me_q) == 1

    even_near, even_far = range(2, half, 2), range(half, n_fine, 2)
    odd_near, odd_far = range(3, half, 2), range(half + 1, n_fine, 2)
    even = [*even_near, *even_far]

    round_out(1)
    enc_rows(1)
    loads[0].wait()
    enc_out(me_q)
    for d in even:
        begin_if(rows_next(d), q_of(d))
    begin(q_of(1))
    pltpu.make_async_copy(kvbuf.at[c, f], kvbuf.at[c, f], load_s.at[1]).wait()
    kv_forward(0)
    for d in even:
        begin_if(rows_next(d), kv_copy(d))
    begin(kv_copy(1))
    row = lax.broadcasted_iota(jnp.int32, (tokens, 3 * tokens), 0)
    col = lax.broadcasted_iota(jnp.int32, (tokens, 3 * tokens), 1)
    for b in range(LOW):
        pos = (two * LOW + b) * tokens + col - tokens
        seen = (jnp.abs(col - tokens - row) <= ROUTED_BLOCK - 1) & (pos >= 0) & (pos < n_seq * tokens)
        band[b] = jnp.where(seen, jnp.float32(0), jnp.float32(NEG))

    loads[4].wait()
    lane_d = lax.broadcasted_iota(jnp.int32, (dec_rows, PAIR), 1)
    for j in range(pairs):
        q = drows[:, j * PAIR:(j + 1) * PAIR].astype(jnp.float32) * (HEAD ** (-0.5))
        swapped = pltpu.roll(q, HEAD, 1)
        both = jnp.concatenate(
            [jnp.where(lane_d < HEAD, q, 0.0), jnp.where(lane_d < HEAD, swapped, 0.0)], axis=0
        )
        dq[2 * j * dec_rows:(2 * j + 2) * dec_rows, :] = both.astype(jnp.bfloat16)

    for r in range(1, n_q - 1):
        round_in(r)
        round_out(r + 1)
    enc_step(1)
    round_in(n_q - 1)
    for t in range(2, n_q):
        enc_rows(t)
    for d in [*odd_near, *even]:
        begin_if(jnp.logical_not(rows_next(d)) if d % 2 == 0 else here >= 0, q_of(d))
    for d in odd_far:
        begin(q_of(d))
    for d in odd_near:
        begin(kv_copy(d))
    enc_turn(me_q)
    enc_side(1)
    for d in even:
        begin_if(jnp.logical_not(rows_next(d)), kv_copy(d))
    for d in range(2, half, 2):
        kv_forward(d)
    for d in range(1, half, 2):
        kv_forward(d)
    for t in range(2, n_q):
        enc_step(t)
    for d in odd_far:
        begin(kv_copy(d))
    begin(swap_copy())
    far = [*range(half, n_fine, 2), *range(half + 1, n_fine, 2)]
    quarter = len(far) // 4
    d_total = heads * dec_rows
    d_chunk = min(256, d_total)

    def dec_step(i):
        rows = pl.ds(pl.multiple_of(i * d_chunk, d_chunk), d_chunk)
        kv = encbuf[...].reshape(n_seq * tokens, PAIR)
        s = dot_t(dq[rows, :], kv)
        e = jnp.exp(s - jnp.max(s, axis=1, keepdims=True))
        total = jnp.sum(e, axis=1, keepdims=True)
        do[rows, :] = dot(e.astype(jnp.bfloat16), kv) / total

    low_half = lax.broadcasted_iota(jnp.int32, (tokens, PAIR), 1) < HEAD
    lane_2 = lax.broadcasted_iota(jnp.int32, (2 * tokens, PAIR), 1)
    keys = n_coarse * half * tokens

    def heavy_scores(j, part):
        q = stacked_pair(qbuf[j], low_half)
        s = dot_t(q, kvbuf[:, pl.ds(part * half, half), 0].reshape(keys, PAIR))
        if has_bias:
            s = s + bias_ref[part, 0:1, :]
        return s

    def heavy_values(part):
        return kvbuf[:, pl.ds(part * half, half), 1].reshape(keys, PAIR)

    def heavy_first(d):
        j = flip(p, d, pairs)
        s = heavy_scores(j, hh)
        peak = jnp.max(s, axis=1, keepdims=True)
        e = jnp.exp(s - peak)
        total = jnp.sum(e, axis=1, keepdims=True)
        acc[j] = dot(e.astype(jnp.bfloat16), heavy_values(hh))
        stat[j] = jnp.where(lane_2 == 0, peak, total)

    def heavy_second(j):
        s = heavy_scores(j, 1 - hh)
        before = stat[j, :, 0:1]
        peak = jnp.maximum(before, jnp.max(s, axis=1, keepdims=True))
        e = jnp.exp(s - peak)
        keep = jnp.exp(before - peak)
        total = stat[j, :, 1:2] * keep + jnp.sum(e, axis=1, keepdims=True)
        o = (acc[j] * keep + dot(e.astype(jnp.bfloat16), heavy_values(1 - hh))) / total
        return jnp.where(low_half, o[:tokens], o[tokens:]).astype(jnp.bfloat16)

    loads[3].wait()
    take(qbuf.at[pl.ds(0, pairs // 2 - 1)], q_r.at[0])
    kv_others(0)
    loop(0, pairs // 2, heavy_first)
    for t in range(2, n_q):
        enc_side(t)
    n_chunk = d_total // d_chunk
    take(qbuf.at[pl.ds(0, pairs // 2)], q_r.at[1])
    loop(pairs // 2, pairs, heavy_first)
    for d in far[0 * quarter:1 * quarter]:
        kv_forward(d)
    take(encbuf.at[pl.ds(0, LOW * (n_coarse - 1))], enc_r.at[2 * n_q])

    loop(0 * n_chunk // 4, 1 * n_chunk // 4, dec_step)
    for d in far[1 * quarter:2 * quarter]:
        kv_forward(d)
    loop(1 * n_chunk // 4, 2 * n_chunk // 4, dec_step)
    for d in far[2 * quarter:3 * quarter]:
        kv_forward(d)
    pltpu.make_async_copy(lk.at[pl.ds(0, 2)], lk.at[pl.ds(0, 2)], load_s.at[4]).wait()
    for side in range(2):
        halo_send(side, lo == side)
    loop(2 * n_chunk // 4, 3 * n_chunk // 4, dec_step)
    for d in far[3 * quarter:4 * quarter]:
        kv_forward(d)
    loop(3 * n_chunk // 4, n_chunk, dec_step)
    for j in range(pairs):
        even = do[2 * j * dec_rows:(2 * j + 1) * dec_rows, :]
        odd = do[(2 * j + 1) * dec_rows:(2 * j + 2) * dec_rows, :]
        dec[c, g, :, j * PAIR:(j + 1) * PAIR] = jnp.where(
            lane_d < HEAD, pltpu.roll(even, HEAD, 1), odd
        ).astype(jnp.bfloat16)
    dec_spread(g, 0)
    take(lk.at[pl.ds(0, 2)], x_r.at[0])
    for side in range(2):
        halo_send(side, lo == 1 - side)
    hop_forward()
    dec_across(g)
    kv_others(1)

    def heavy_out(i):
        d = pairs - 1 - i
        j = flip(p, d, pairs)
        osend[j] = heavy_second(j)
        o_copy(d).start()

    loop(0, pairs // 2, heavy_out)
    dec_wave(1)
    loop(pairs // 2, pairs - 1, heavy_out)
    orecv[p] = heavy_second(p)

    take(lq.at[1 - lo], x_r.at[1])
    loads[7].wait()
    for side in range(2):
        @pl.when(has_peer[side])
        def _():
            take(lk.at[pl.ds(0, 2)], h_r.at[1 - side])

        @pl.when(jnp.logical_not(has_peer[side]))
        def _():
            lk[3 * side] = jnp.zeros((tokens, wide), jnp.bfloat16)
            lv[3 * side] = jnp.zeros((tokens, wide), jnp.bfloat16)

    def light_of(b, j):
        cols = cols_of(j)
        q = stacked_pair(lq[b, :, cols], low_half)
        mask = band[b]
        s = dot_t(q, lk[pl.ds(b, 3), :, cols].reshape(3 * tokens, PAIR))
        s = s + jnp.concatenate([mask, mask], axis=0)
        e = jnp.exp(s - jnp.max(s, axis=1, keepdims=True))
        total = jnp.sum(e, axis=1, keepdims=True)
        o = dot(e.astype(jnp.bfloat16), lv[pl.ds(b, 3), :, cols].reshape(3 * tokens, PAIR)) / total
        return jnp.where(low_half, o[:tokens], o[tokens:])

    def light_away(j):
        lsend[j] = light_of(1 - lo, j).astype(jnp.bfloat16)
        light_back(j).start()

    def light_home(j):
        lown[:, cols_of(j)] = light_of(lo, j)

    loop(0, pairs_half, light_away)
    for steps in range(2, len(bits) + 1):
        dec_wave(steps)
    loop(0, pairs_half, light_home)

    take(orecv.at[pl.ds(0, pairs - 1)], o_r)

    def join_home(j):
        pair = lo * pairs_half + j
        heavy = orecv[pair].astype(jnp.float32)
        out[:, cols_of(pair)] = (lown[:, cols_of(j)] + heavy).astype(jnp.bfloat16)

    def join_away(j):
        pair = (1 - lo) * pairs_half + j
        heavy = orecv[pair].astype(jnp.float32)
        out[:, cols_of(pair)] = (lrecv[j].astype(jnp.float32) + heavy).astype(jnp.bfloat16)

    loop(0, pairs_half, join_home)
    take(lrecv, lo_r)
    loop(0, pairs_half, join_away)

    take(dec.at[pl.ds(0, n_coarse - 1)], dec_r.at[half])
    drain(encbuf.at[0, pl.ds(0, n_q - 1)], enc_s)
    drain(encbuf.at[0], ey_s)
    drain(encbuf.at[pl.ds(0, LOW * (n_coarse - 1))], ex_s)
    drain(qbuf.at[pl.ds(0, pairs - 1)], q_s)
    drain(osend.at[pl.ds(0, pairs - 1)], o_s)
    drain(kvbuf.at[0, pl.ds(0, n_fine - 1)], kv_s)
    drain(kvbuf.at[pl.ds(0, n_coarse - 1)], kx_s)
    drain(lk.at[pl.ds(0, 3)], x_s)
    drain(lsend, lo_s)
    for side in range(2):
        @pl.when(has_peer[side])
        def _():
            drain(lk.at[pl.ds(0, 2)], h_s.at[side])

        @pl.when(hops_here[side])
        def _():
            drain(hop, hop_s)
    for k in range(len(bits) + n_coarse - 1):
        drain(dec.at[0, pl.ds(0, min(2 ** k, half))], dec_s.at[k])


def local(
    q_light, k_light, v_light, q_heavy, k_heavy, v_heavy, enc_kv, dec_queries, query_ids, key_ids
):
    _, tokens, width = q_light.shape
    n_coarse = lax.axis_size("coarse")
    n_fine = lax.axis_size("fine")
    n_seq = n_coarse * n_fine
    n_q = n_fine // LOW
    n_kv = n_coarse * LOW
    half = n_fine // 2
    heads = width // HEAD
    pairs = heads // 2
    count = dec_queries.shape[1]
    dec_rows = count // (n_coarse * half)
    n_bits = half.bit_length() - 1
    mine = dec_queries.reshape(n_coarse, half, dec_rows, width)
    args = [q_light[0], k_light[0], v_light[0], q_heavy[0], k_heavy[0], v_heavy[0], enc_kv[0], mine]
    args = [pltpu.with_memory_space_constraint(a, pltpu.HBM) for a in args]
    has_bias = key_ids.shape[1] != n_seq
    keys = n_coarse * half * tokens
    if has_bias:
        blocks = jnp.arange(n_seq, dtype=jnp.int32).reshape(n_coarse, 2, half).transpose(1, 0, 2)
        listed = jnp.any(blocks[..., None] == key_ids[0], axis=-1).reshape(2, 1, n_coarse * half)
        bias = jnp.repeat(jnp.where(listed, 0.0, NEG).astype(jnp.float32), tokens, axis=2)
        args.append(jnp.broadcast_to(bias, (2, 8, keys)))
    bf16, f32 = jnp.bfloat16, jnp.float32
    dma = pltpu.SemaphoreType.DMA
    vmem = pl.BlockSpec(memory_space=pltpu.VMEM)
    hbm = pl.BlockSpec(memory_space=pltpu.HBM)
    wide = width // LOW
    encoded, decoded = pl.pallas_call(
        functools.partial(kernel, (n_coarse, n_fine, tokens, width, dec_rows), has_bias),
        out_shape=(
            jax.ShapeDtypeStruct((tokens, width), bf16),
            jax.ShapeDtypeStruct((n_coarse, half, dec_rows, width), bf16),
        ),
        in_specs=[hbm] * 8 + [vmem] * (len(args) - 8),
        out_specs=(vmem, vmem),
        scratch_shapes=[
            pltpu.VMEM((n_kv, n_q, tokens, PAIR), bf16),
            pltpu.VMEM((dec_rows, width), bf16),
            pltpu.VMEM((heads * dec_rows, PAIR), bf16),
            pltpu.VMEM((heads * dec_rows, PAIR), f32),
            pltpu.VMEM((pairs, tokens, PAIR), bf16),
            pltpu.VMEM((n_coarse, n_fine, 2, tokens, PAIR), bf16),
            pltpu.VMEM((pairs, 2 * tokens, PAIR), f32),
            pltpu.VMEM((pairs, 2 * tokens, PAIR), f32),
            pltpu.VMEM((pairs, tokens, PAIR), bf16),
            pltpu.VMEM((pairs, tokens, PAIR), bf16),
            pltpu.VMEM((2, tokens, wide), bf16),
            pltpu.VMEM((4, tokens, wide), bf16),
            pltpu.VMEM((4, tokens, wide), bf16),
            pltpu.VMEM((tokens, wide), bf16),
            pltpu.VMEM((tokens, wide), f32),
            pltpu.VMEM((pairs // LOW, tokens, PAIR), bf16),
            pltpu.VMEM((pairs // LOW, tokens, PAIR), bf16),
            pltpu.VMEM((2, tokens, 3 * tokens), f32),
            dma((6,)),
            dma, dma((2 * n_q + 1,)), dma, dma,
            dma, dma((2,)),
            dma, dma((n_fine + 2,)), dma,
            pltpu.SemaphoreType.REGULAR((n_q,)),
            dma, dma((2,)),
            dma((2,)), dma((2,)),
            dma, dma,
            dma, dma,
            dma, dma,
            dma((n_bits + n_coarse - 1,)), dma((half + 1,)),
        ],
        compiler_params=pltpu.CompilerParams(
            collective_id=0, has_side_effects=True, vmem_limit_bytes=32 * 1024 * 1024
        ),
    )(*args)
    return encoded[None], decoded.reshape(1, count, width)


def solution(mesh):
    rows = P("doc", ("coarse", "fine"), None)
    placed = (rows,) * 7 + (P("doc", None, None), P("doc", None), P("doc", None))
    return jax.shard_map(
        local,
        mesh=mesh,
        in_specs=placed,
        out_specs=(rows, P("doc", None, None)),
        check_vma=False,
    )
```

```python
import functools

import jax
import jax.numpy as jnp
from jax import lax
from jax.experimental import pallas as pl
from jax.experimental.pallas import tpu as pltpu
from jax.sharding import PartitionSpec as P

HEAD = 64
PAIR = 2 * HEAD
ROUTED_BLOCK = 128
LOW = 2
MESH = pl.DeviceIdType.MESH
NEG = -1e30


def dot_t(a, b):
    return lax.dot_general(a, b, (((1,), (1,)), ((), ())), preferred_element_type=jnp.float32)


def dot(a, b):
    return jnp.dot(a, b, preferred_element_type=jnp.float32)


def stacked_pair(q, low_half):
    q = q * jnp.asarray(HEAD ** (-0.5), q.dtype)
    zero = jnp.zeros_like(q)
    return jnp.concatenate([jnp.where(low_half, q, zero), jnp.where(low_half, zero, q)], axis=0)


def flip(v, d, n):
    out, bit = 0, 1
    while bit < n:
        if isinstance(d, int):
            on = (d // bit) % 2
        else:
            on = lax.rem(lax.div(d, bit), 2)
        out = out + lax.rem(lax.div(v, bit) + on, 2) * bit
        bit *= 2
    return out


def kernel(dims, has_bias, *refs):
    n_coarse, n_fine, tokens, width, dec_rows = dims
    n_seq = n_coarse * n_fine
    n_q = n_fine // LOW
    n_kv = n_coarse * LOW
    n_pair_seq = n_seq // LOW
    half = n_fine // 2
    heads = width // HEAD
    pairs = heads // 2
    share = n_fine // pairs
    wide = width // LOW
    pairs_half = pairs // LOW
    refs = list(refs)
    ql, kl, vl, qh, kh, vh, enc, decq = refs[:8]
    bias_ref = refs[8] if has_bias else None
    (out, dec, encbuf, drows, dq, do, qbuf, kvbuf, acc, stat, osend, orecv,
     lq, lk, lv, hop, lown, lsend, lrecv, band,
     load_s, enc_s, enc_r, ey_s, ex_s, q_s, q_r, kv_s, kv_r, kx_s,
     far_s, x_s, x_r, h_s, h_r, hop_s, hop_r, o_s, o_r, lo_s, lo_r, dec_s, dec_r) = refs[8 + has_bias:]

    c = lax.axis_index("coarse")
    f = lax.axis_index("fine")
    here = c * n_fine + f
    me_q = lax.div(f, LOW)
    lo = lax.rem(f, LOW)
    me_kv = c * LOW + lo
    p = lax.div(f, share)
    s_me = lax.rem(f, share)
    hh = lax.div(f, half)
    g = lax.rem(f, half)
    two = lax.div(here, LOW)

    def remote(src, dst, ssem, rsem, device):
        return pltpu.make_async_remote_copy(
            src_ref=src, dst_ref=dst, send_sem=ssem, recv_sem=rsem,
            device_id=device, device_id_type=MESH,
        )

    def take(ref, sem):
        remote(ref, ref, sem, sem, at(c, f)).wait_recv()

    def drain(ref, sem):
        remote(ref, ref, sem, sem, at(c, f)).wait_send()

    def up(me, d, n):
        return lax.rem(me + d, n)

    def down(me, d, n):
        return lax.rem(me + n - d, n)

    def at(cc, ff):
        return {"coarse": cc, "fine": ff}

    def cols_of(pair):
        return pl.ds(pl.multiple_of(pair * PAIR, PAIR), PAIR)

    def side_of(which):
        return pl.ds(pl.multiple_of(which * wide, PAIR), wide)

    def loop(start, stop, body):
        def step(d, carry):
            body(d)
            return carry
        lax.fori_loop(start, stop, step, 0)

    def loop_two(start, stop, work, save):
        def step(i, carry):
            d = start + 2 * i
            first, second = work(d), work(d + 1)
            save(d, first)
            save(d + 1, second)
            return carry
        lax.fori_loop(0, (stop - start) // 2, step, 0)
        if (stop - start) % 2:
            save(stop - 1, work(stop - 1))

    def begin(copies):
        for copy in copies:
            copy.start()

    def begin_if(cond, copies):
        @pl.when(cond)
        def _():
            begin(copies)

    loads = [
        pltpu.make_async_copy(enc, encbuf.at[me_kv, me_q], load_s.at[0]),
        pltpu.make_async_copy(kh.at[:, cols_of(p)], kvbuf.at[c, f, 0], load_s.at[1]),
        pltpu.make_async_copy(vh.at[:, cols_of(p)], kvbuf.at[c, f, 1], load_s.at[1]),
        pltpu.make_async_copy(qh.at[:, cols_of(p)], qbuf.at[p], load_s.at[2]),
        pltpu.make_async_copy(decq.at[c, g], drows, load_s.at[3]),
        pltpu.make_async_copy(kl.at[:, side_of(lo)], lk.at[1 + lo], load_s.at[4]),
        pltpu.make_async_copy(vl.at[:, side_of(lo)], lv.at[1 + lo], load_s.at[4]),
        pltpu.make_async_copy(ql.at[:, side_of(lo)], lq.at[lo], load_s.at[5]),
    ]
    for copy in loads:
        copy.start()

    barrier = pltpu.get_barrier_semaphore()

    has_up = me_q < n_q - 1
    has_down = me_q > 0
    n_near = n_coarse + has_up.astype(jnp.int32) + has_down.astype(jnp.int32)

    def greet(sem):
        def say(device):
            pl.semaphore_signal(sem, inc=1, device_id=device, device_id_type=MESH)

        say(at(c, f + 1 - 2 * lo))
        for e in range(1, n_coarse):
            say(at(up(c, e, n_coarse), f))

        @pl.when(has_up)
        def _():
            say(at(c, jnp.minimum(f + LOW, n_fine - 1)))

        @pl.when(has_down)
        def _():
            say(at(c, jnp.maximum(f - LOW, 0)))

    greet(barrier)
    pl.semaphore_wait(barrier, n_near)

    def round_out(r):
        greet(far_s.at[r])

    def round_in(r):
        pl.semaphore_wait(far_s.at[r], n_near)

    def enc_row(way):
        peer = jnp.clip(me_q + way, 0, n_q - 1)
        return remote(
            enc, encbuf.at[me_kv, me_q], enc_s, enc_r.at[me_q], at(c, peer * LOW + lo)
        )

    def enc_mate(block):
        part = encbuf.at[me_kv, block]
        return remote(part, part, ey_s, enc_r.at[n_q + block], at(c, f + 1 - 2 * lo))

    def enc_across(low, block, e):
        part = encbuf.at[c * LOW + low, block]
        return remote(part, part, ex_s, enc_r.at[2 * n_q], at(up(c, e, n_coarse), f))

    def enc_out(block):
        enc_mate(block).start()
        for e in range(1, n_coarse):
            enc_across(lo, block, e).start()

    def enc_at(t):
        for way in (t, -t):
            row = me_q + way
            yield way, jnp.clip(row, 0, n_q - 1), (row >= 0) & (row < n_q)

    def enc_rows(t):
        for way, row, there in enc_at(t):
            begin_if(there, (enc_row(way),))

    def enc_step(t):
        for way, row, there in enc_at(t):
            @pl.when(there)
            def _():
                take(encbuf.at[me_kv, row], enc_r.at[row])
                enc_out(row)

    def enc_turn(block):
        take(encbuf.at[c * LOW + 1 - lo, block], enc_r.at[n_q + block])
        for e in range(1, n_coarse):
            enc_across(1 - lo, block, e).start()

    def enc_side(t):
        for way, row, there in enc_at(t):
            @pl.when(there)
            def _():
                enc_turn(row)

    def q_copy(d):
        to = flip(p, d, pairs)
        return remote(qh.at[:, cols_of(to)], qbuf.at[p], q_s, q_r.at[int(d >= pairs // 2)], at(c, to * share + s_me))

    def kv_copy(d):
        to = flip(f, d, n_fine)
        col = cols_of(lax.div(to, share))
        return (
            remote(kh.at[:, col], kvbuf.at[c, f, 0], kv_s, kv_r.at[f], at(c, to)),
            remote(vh.at[:, col], kvbuf.at[c, f, 1], kv_s, kv_r.at[f], at(c, to)),
        )

    def kv_forward(d):
        src = flip(f, d, n_fine)
        block = kvbuf.at[c, src]
        if d:
            take(block, kv_r.at[src])
        for e in range(1, n_coarse):
            remote(block, block, kx_s, kv_r.at[n_fine + int(d >= half)], at(up(c, e, n_coarse), f)).start()

    def kv_others(far_half):
        take(kvbuf.at[pl.ds(0, n_coarse - 1), pl.ds(0, half)], kv_r.at[n_fine + far_half])

    def o_copy(d):
        to = flip(p, d, pairs)
        return remote(osend.at[to], orecv.at[p], o_s, o_r, at(c, to * share + s_me))

    mate = at(c, f + 1 - 2 * lo)

    def swap_copy():
        cols = side_of(1 - lo)
        return (
            remote(kl.at[:, cols], lk.at[1 + lo], x_s, x_r.at[0], mate),
            remote(vl.at[:, cols], lv.at[1 + lo], x_s, x_r.at[0], mate),
            remote(ql.at[:, cols], lq.at[lo], x_s, x_r.at[1], mate),
        )

    def halo_copy(side):
        peer = jnp.clip(two + 2 * side - 1, 0, n_pair_seq - 1) * LOW + lo
        device = at(lax.div(peer, n_fine), lax.rem(peer, n_fine))
        slot = 3 - 3 * side
        return (
            remote(lk.at[1 + side], lk.at[slot], h_s.at[side], h_r.at[side], device),
            remote(lv.at[1 + side], lv.at[slot], h_s.at[side], h_r.at[side], device),
        )

    has_peer = [two > 0, two < n_pair_seq - 1]
    at_edge = [me_q == 0, me_q == n_q - 1]

    def hop_copy(side):
        peer = jnp.clip(c + 2 * side - 1, 0, n_coarse - 1)
        return remote(lv.at[1 + side], hop, h_s.at[side], hop_r, at(peer, f))

    def hop_on(side):
        end = (1 - side) * (n_q - 1)
        slot = 3 - 3 * side
        return remote(hop, lv.at[slot], hop_s, h_r.at[side], at(c, end * LOW + lo))

    hops_here = [at_edge[0] & (c < n_coarse - 1), at_edge[1] & (c > 0)]

    def halo_send(side, mine):
        go = mine & has_peer[side]
        keys, values = halo_copy(side)

        @pl.when(go)
        def _():
            keys.start()

        @pl.when(go & jnp.logical_not(at_edge[side]))
        def _():
            values.start()

        @pl.when(go & at_edge[side])
        def _():
            hop_copy(side).start()

    def hop_forward():
        for side in range(2):
            @pl.when(hops_here[side])
            def _():
                hop_copy(side).wait_recv()
                hop_on(side).start()

    def light_back(j):
        return remote(lsend.at[j], lrecv.at[j], lo_s, lo_r, mate)

    bits = []
    bit = half // 2
    while bit:
        bits.append(bit)
        bit //= 2

    def dec_copy(block, k):
        mine = dec.at[c, block]
        if k < len(bits):
            peer = at(c, hh * half + flip(g, bits[k], half))
        else:
            peer = at(up(c, k - len(bits) + 1, n_coarse), f)
        return remote(mine, mine, dec_s.at[k], dec_r.at[block if k < len(bits) else half], peer)

    def dec_spread(block, first):
        for k in range(first, len(bits)):
            dec_copy(block, k).start()

    def dec_across(block):
        for k in range(len(bits), len(bits) + n_coarse - 1):
            dec_copy(block, k).start()

    def dec_wave(steps):
        for x in range(1, half):
            if bin(x).count("1") == steps:
                block = flip(g, x, half)
                last = bits.index(x & -x)
                take(dec.at[c, block], dec_r.at[block])
                dec_spread(block, last + 1)
                dec_across(block)

    def q_of(d):
        return (q_copy(d // share),) if d % share == 0 else ()

    def rows_next(d):
        return jnp.abs(lax.div(flip(f, d, n_fine), LOW) - me_q) == 1

    even_near, even_far = range(2, half, 2), range(half, n_fine, 2)
    odd_near, odd_far = range(3, half, 2), range(half + 1, n_fine, 2)
    even = [*even_near, *even_far]

    round_out(1)
    enc_rows(1)
    loads[0].wait()
    enc_out(me_q)
    for d in even:
        begin_if(rows_next(d), q_of(d))
    begin(q_of(1))
    pltpu.make_async_copy(kvbuf.at[c, f], kvbuf.at[c, f], load_s.at[1]).wait()
    kv_forward(0)
    for d in even:
        begin_if(rows_next(d), kv_copy(d))
    begin(kv_copy(1))
    row = lax.broadcasted_iota(jnp.int32, (tokens, 3 * tokens), 0)
    col = lax.broadcasted_iota(jnp.int32, (tokens, 3 * tokens), 1)
    for b in range(LOW):
        pos = (two * LOW + b) * tokens + col - tokens
        seen = (jnp.abs(col - tokens - row) <= ROUTED_BLOCK - 1) & (pos >= 0) & (pos < n_seq * tokens)
        band[b] = jnp.where(seen, jnp.float32(0), jnp.float32(NEG))

    loads[4].wait()
    lane_d = lax.broadcasted_iota(jnp.int32, (dec_rows, PAIR), 1)
    for j in range(pairs):
        q = drows[:, j * PAIR:(j + 1) * PAIR].astype(jnp.float32) * (HEAD ** (-0.5))
        swapped = pltpu.roll(q, HEAD, 1)
        both = jnp.concatenate(
            [jnp.where(lane_d < HEAD, q, 0.0), jnp.where(lane_d < HEAD, swapped, 0.0)], axis=0
        )
        dq[2 * j * dec_rows:(2 * j + 2) * dec_rows, :] = both.astype(jnp.bfloat16)

    for r in range(1, n_q - 1):
        round_in(r)
        round_out(r + 1)
    enc_step(1)
    round_in(n_q - 1)
    for t in range(2, n_q):
        enc_rows(t)
    for d in [*odd_near, *even]:
        begin_if(jnp.logical_not(rows_next(d)) if d % 2 == 0 else here >= 0, q_of(d))
    for d in odd_far:
        begin(q_of(d))
    for d in odd_near:
        begin(kv_copy(d))
    enc_turn(me_q)
    enc_side(1)
    for d in even:
        begin_if(jnp.logical_not(rows_next(d)), kv_copy(d))
    for d in range(2, half, 2):
        kv_forward(d)
    for d in range(1, half, 2):
        kv_forward(d)
    for t in range(2, n_q):
        enc_step(t)
    for d in odd_far:
        begin(kv_copy(d))
    begin(swap_copy())
    far = [*range(half, n_fine, 2), *range(half + 1, n_fine, 2)]
    quarter = len(far) // 4
    d_total = heads * dec_rows
    d_chunk = min(256, d_total)

    def dec_step(i):
        rows = pl.ds(pl.multiple_of(i * d_chunk, d_chunk), d_chunk)
        kv = encbuf[...].reshape(n_seq * tokens, PAIR)
        s = dot_t(dq[rows, :], kv)
        e = jnp.exp(s - jnp.max(s, axis=1, keepdims=True))
        total = jnp.sum(e, axis=1, keepdims=True)
        do[rows, :] = dot(e.astype(jnp.bfloat16), kv) / total

    low_half = lax.broadcasted_iota(jnp.int32, (tokens, PAIR), 1) < HEAD
    lane_2 = lax.broadcasted_iota(jnp.int32, (2 * tokens, PAIR), 1)
    keys = n_coarse * half * tokens

    def heavy_scores(j, part):
        q = stacked_pair(qbuf[j], low_half)
        s = dot_t(q, kvbuf[:, pl.ds(part * half, half), 0].reshape(keys, PAIR))
        if has_bias:
            s = s + bias_ref[part, 0:1, :]
        return s

    def heavy_values(part):
        return kvbuf[:, pl.ds(part * half, half), 1].reshape(keys, PAIR)

    def heavy_first(d):
        j = flip(p, d, pairs)
        s = heavy_scores(j, hh)
        peak = jnp.max(s, axis=1, keepdims=True)
        e = jnp.exp(s - peak)
        total = jnp.sum(e, axis=1, keepdims=True)
        return j, dot(e.astype(jnp.bfloat16), heavy_values(hh)), peak, total

    def heavy_keep(d, result):
        j, o, peak, total = result
        acc[j] = o
        stat[j] = jnp.where(lane_2 == 0, peak, total)

    def heavy_second(j):
        s = heavy_scores(j, 1 - hh)
        before = stat[j, :, 0:1]
        peak = jnp.maximum(before, jnp.max(s, axis=1, keepdims=True))
        e = jnp.exp(s - peak)
        keep = jnp.exp(before - peak)
        total = stat[j, :, 1:2] * keep + jnp.sum(e, axis=1, keepdims=True)
        o = (acc[j] * keep + dot(e.astype(jnp.bfloat16), heavy_values(1 - hh))) / total
        return jnp.where(low_half, o[:tokens], o[tokens:]).astype(jnp.bfloat16)

    loads[3].wait()
    take(qbuf.at[pl.ds(0, pairs // 2 - 1)], q_r.at[0])
    kv_others(0)
    loop_two(0, pairs // 2, heavy_first, heavy_keep)
    for t in range(2, n_q):
        enc_side(t)
    n_chunk = d_total // d_chunk
    n_chunk = d_total // d_chunk
    take(qbuf.at[pl.ds(0, pairs // 2)], q_r.at[1])
    loop_two(pairs // 2, pairs, heavy_first, heavy_keep)
    for d in far[0 * quarter:1 * quarter]:
        kv_forward(d)
    take(encbuf.at[pl.ds(0, LOW * (n_coarse - 1))], enc_r.at[2 * n_q])
    pltpu.make_async_copy(lk.at[pl.ds(0, 2)], lk.at[pl.ds(0, 2)], load_s.at[4]).wait()
    for side in range(2):
        halo_send(side, lo == side)
    loop(0 * n_chunk // 4, 1 * n_chunk // 4, dec_step)
    for d in far[1 * quarter:2 * quarter]:
        kv_forward(d)
    loop(1 * n_chunk // 4, 2 * n_chunk // 4, dec_step)
    for d in far[2 * quarter:3 * quarter]:
        kv_forward(d)
    loop(2 * n_chunk // 4, 3 * n_chunk // 4, dec_step)
    for d in far[3 * quarter:4 * quarter]:
        kv_forward(d)
    loop(3 * n_chunk // 4, n_chunk, dec_step)
    for j in range(pairs):
        even = do[2 * j * dec_rows:(2 * j + 1) * dec_rows, :]
        odd = do[(2 * j + 1) * dec_rows:(2 * j + 2) * dec_rows, :]
        dec[c, g, :, j * PAIR:(j + 1) * PAIR] = jnp.where(
            lane_d < HEAD, pltpu.roll(even, HEAD, 1), odd
        ).astype(jnp.bfloat16)
    dec_spread(g, 0)
    take(lk.at[pl.ds(0, 2)], x_r.at[0])
    for side in range(2):
        halo_send(side, lo == 1 - side)
    hop_forward()
    dec_across(g)
    kv_others(1)

    def heavy_end(i):
        j = flip(p, pairs - 1 - i, pairs)
        return j, heavy_second(j)

    def heavy_out(i, result):
        osend[result[0]] = result[1]
        o_copy(pairs - 1 - i).start()

    loop_two(0, pairs // 2, heavy_end, heavy_out)
    dec_wave(1)
    loop_two(pairs // 2, pairs - 2, heavy_end, heavy_out)
    near, home = heavy_end(pairs - 2), heavy_end(pairs - 1)
    heavy_out(pairs - 2, near)
    orecv[p] = home[1]

    take(lq.at[1 - lo], x_r.at[1])
    loads[7].wait()
    for side in range(2):
        @pl.when(has_peer[side])
        def _():
            take(lk.at[pl.ds(0, 2)], h_r.at[1 - side])

        @pl.when(jnp.logical_not(has_peer[side]))
        def _():
            lk[3 * side] = jnp.zeros((tokens, wide), jnp.bfloat16)
            lv[3 * side] = jnp.zeros((tokens, wide), jnp.bfloat16)

    def light_of(b, j):
        cols = cols_of(j)
        q = stacked_pair(lq[b, :, cols], low_half)
        mask = band[b]
        s = dot_t(q, lk[pl.ds(b, 3), :, cols].reshape(3 * tokens, PAIR))
        s = s + jnp.concatenate([mask, mask], axis=0)
        e = jnp.exp(s - jnp.max(s, axis=1, keepdims=True))
        total = jnp.sum(e, axis=1, keepdims=True)
        o = dot(e.astype(jnp.bfloat16), lv[pl.ds(b, 3), :, cols].reshape(3 * tokens, PAIR)) / total
        return jnp.where(low_half, o[:tokens], o[tokens:])

    def light_away(j, o):
        lsend[j] = o.astype(jnp.bfloat16)
        light_back(j).start()

    def light_home(j, o):
        lown[:, cols_of(j)] = o

    loop_two(0, pairs_half, lambda j: light_of(1 - lo, j), light_away)
    for steps in range(2, len(bits) + 1):
        dec_wave(steps)
    loop_two(0, pairs_half, lambda j: light_of(lo, j), light_home)

    take(orecv.at[pl.ds(0, pairs - 1)], o_r)

    def join_home(j):
        pair = lo * pairs_half + j
        heavy = orecv[pair].astype(jnp.float32)
        out[:, cols_of(pair)] = (lown[:, cols_of(j)] + heavy).astype(jnp.bfloat16)

    def join_away(j):
        pair = (1 - lo) * pairs_half + j
        heavy = orecv[pair].astype(jnp.float32)
        out[:, cols_of(pair)] = (lrecv[j].astype(jnp.float32) + heavy).astype(jnp.bfloat16)

    loop(0, pairs_half, join_home)
    take(lrecv, lo_r)
    loop(0, pairs_half, join_away)

    take(dec.at[pl.ds(0, n_coarse - 1)], dec_r.at[half])
    drain(encbuf.at[0, pl.ds(0, n_q - 1)], enc_s)
    drain(encbuf.at[0], ey_s)
    drain(encbuf.at[pl.ds(0, LOW * (n_coarse - 1))], ex_s)
    drain(qbuf.at[pl.ds(0, pairs - 1)], q_s)
    drain(osend.at[pl.ds(0, pairs - 1)], o_s)
    drain(kvbuf.at[0, pl.ds(0, n_fine - 1)], kv_s)
    drain(kvbuf.at[pl.ds(0, n_coarse - 1)], kx_s)
    drain(lk.at[pl.ds(0, 3)], x_s)
    drain(lsend, lo_s)
    for side in range(2):
        @pl.when(has_peer[side])
        def _():
            drain(lk.at[pl.ds(0, 2)], h_s.at[side])

        @pl.when(hops_here[side])
        def _():
            drain(hop, hop_s)
    for k in range(len(bits) + n_coarse - 1):
        drain(dec.at[0, pl.ds(0, min(2 ** k, half))], dec_s.at[k])


def local(
    q_light, k_light, v_light, q_heavy, k_heavy, v_heavy, enc_kv, dec_queries, query_ids, key_ids
):
    _, tokens, width = q_light.shape
    n_coarse = lax.axis_size("coarse")
    n_fine = lax.axis_size("fine")
    n_seq = n_coarse * n_fine
    n_q = n_fine // LOW
    n_kv = n_coarse * LOW
    half = n_fine // 2
    heads = width // HEAD
    pairs = heads // 2
    count = dec_queries.shape[1]
    dec_rows = count // (n_coarse * half)
    n_bits = half.bit_length() - 1
    mine = dec_queries.reshape(n_coarse, half, dec_rows, width)
    args = [q_light[0], k_light[0], v_light[0], q_heavy[0], k_heavy[0], v_heavy[0], enc_kv[0], mine]
    args = [pltpu.with_memory_space_constraint(a, pltpu.HBM) for a in args]
    has_bias = key_ids.shape[1] != n_seq
    keys = n_coarse * half * tokens
    if has_bias:
        blocks = jnp.arange(n_seq, dtype=jnp.int32).reshape(n_coarse, 2, half).transpose(1, 0, 2)
        listed = jnp.any(blocks[..., None] == key_ids[0], axis=-1).reshape(2, 1, n_coarse * half)
        bias = jnp.repeat(jnp.where(listed, 0.0, NEG).astype(jnp.float32), tokens, axis=2)
        args.append(jnp.broadcast_to(bias, (2, 8, keys)))
    bf16, f32 = jnp.bfloat16, jnp.float32
    dma = pltpu.SemaphoreType.DMA
    vmem = pl.BlockSpec(memory_space=pltpu.VMEM)
    hbm = pl.BlockSpec(memory_space=pltpu.HBM)
    wide = width // LOW
    encoded, decoded = pl.pallas_call(
        functools.partial(kernel, (n_coarse, n_fine, tokens, width, dec_rows), has_bias),
        out_shape=(
            jax.ShapeDtypeStruct((tokens, width), bf16),
            jax.ShapeDtypeStruct((n_coarse, half, dec_rows, width), bf16),
        ),
        in_specs=[hbm] * 8 + [vmem] * (len(args) - 8),
        out_specs=(vmem, vmem),
        scratch_shapes=[
            pltpu.VMEM((n_kv, n_q, tokens, PAIR), bf16),
            pltpu.VMEM((dec_rows, width), bf16),
            pltpu.VMEM((heads * dec_rows, PAIR), bf16),
            pltpu.VMEM((heads * dec_rows, PAIR), f32),
            pltpu.VMEM((pairs, tokens, PAIR), bf16),
            pltpu.VMEM((n_coarse, n_fine, 2, tokens, PAIR), bf16),
            pltpu.VMEM((pairs, 2 * tokens, PAIR), f32),
            pltpu.VMEM((pairs, 2 * tokens, PAIR), f32),
            pltpu.VMEM((pairs, tokens, PAIR), bf16),
            pltpu.VMEM((pairs, tokens, PAIR), bf16),
            pltpu.VMEM((2, tokens, wide), bf16),
            pltpu.VMEM((4, tokens, wide), bf16),
            pltpu.VMEM((4, tokens, wide), bf16),
            pltpu.VMEM((tokens, wide), bf16),
            pltpu.VMEM((tokens, wide), f32),
            pltpu.VMEM((pairs // LOW, tokens, PAIR), bf16),
            pltpu.VMEM((pairs // LOW, tokens, PAIR), bf16),
            pltpu.VMEM((2, tokens, 3 * tokens), f32),
            dma((6,)),
            dma, dma((2 * n_q + 1,)), dma, dma,
            dma, dma((2,)),
            dma, dma((n_fine + 2,)), dma,
            pltpu.SemaphoreType.REGULAR((n_q,)),
            dma, dma((2,)),
            dma((2,)), dma((2,)),
            dma, dma,
            dma, dma,
            dma, dma,
            dma((n_bits + n_coarse - 1,)), dma((half + 1,)),
        ],
        compiler_params=pltpu.CompilerParams(
            collective_id=0, has_side_effects=True, vmem_limit_bytes=32 * 1024 * 1024
        ),
    )(*args)
    return encoded[None], decoded.reshape(1, count, width)


def solution(mesh):
    rows = P("doc", ("coarse", "fine"), None)
    placed = (rows,) * 7 + (P("doc", None, None), P("doc", None), P("doc", None))
    return jax.shard_map(
        local,
        mesh=mesh,
        in_specs=placed,
        out_specs=(rows, P("doc", None, None)),
        check_vma=False,
    )
```

```python
import functools

import jax
import jax.numpy as jnp
from jax import lax
from jax.experimental import pallas as pl
from jax.experimental.pallas import tpu as pltpu
from jax.sharding import PartitionSpec as P

HEAD = 64
PAIR = 2 * HEAD
ROUTED_BLOCK = 128
LOW = 2
MESH = pl.DeviceIdType.MESH
NEG = -1e30


def dot_t(a, b):
    return lax.dot_general(a, b, (((1,), (1,)), ((), ())), preferred_element_type=jnp.float32)


def dot(a, b):
    return jnp.dot(a, b, preferred_element_type=jnp.float32)


def stacked_pair(q, low_half):
    q = q * jnp.asarray(HEAD ** (-0.5), q.dtype)
    zero = jnp.zeros_like(q)
    return jnp.concatenate([jnp.where(low_half, q, zero), jnp.where(low_half, zero, q)], axis=0)


def flip(v, d, n):
    out, bit = 0, 1
    while bit < n:
        if isinstance(d, int):
            on = (d // bit) % 2
        else:
            on = lax.rem(lax.div(d, bit), 2)
        out = out + lax.rem(lax.div(v, bit) + on, 2) * bit
        bit *= 2
    return out


def kernel(dims, has_bias, *refs):
    n_coarse, n_fine, tokens, width, dec_rows = dims
    n_seq = n_coarse * n_fine
    n_q = n_fine // LOW
    n_kv = n_coarse * LOW
    n_pair_seq = n_seq // LOW
    half = n_fine // 2
    heads = width // HEAD
    pairs = heads // 2
    share = n_fine // pairs
    wide = width // LOW
    pairs_half = pairs // LOW
    refs = list(refs)
    ql, kl, vl, qh, kh, vh, enc, decq = refs[:8]
    bias_ref = refs[8] if has_bias else None
    (out, dec, encbuf, drows, dq, do, qbuf, kvbuf, acc, stat, osend, orecv,
     lq, lk, lv, hop, lown, lsend, lrecv, band,
     load_s, enc_s, enc_r, ey_s, ex_s, q_s, q_r, kv_s, kv_r, kx_s,
     far_s, x_s, x_r, h_s, h_r, hop_s, hop_r, o_s, o_r, lo_s, lo_r, dec_s, dec_r) = refs[8 + has_bias:]

    c = lax.axis_index("coarse")
    f = lax.axis_index("fine")
    here = c * n_fine + f
    me_q = lax.div(f, LOW)
    lo = lax.rem(f, LOW)
    me_kv = c * LOW + lo
    p = lax.div(f, share)
    s_me = lax.rem(f, share)
    hh = lax.div(f, half)
    g = lax.rem(f, half)
    two = lax.div(here, LOW)

    def remote(src, dst, ssem, rsem, device):
        return pltpu.make_async_remote_copy(
            src_ref=src, dst_ref=dst, send_sem=ssem, recv_sem=rsem,
            device_id=device, device_id_type=MESH,
        )

    def take(ref, sem):
        remote(ref, ref, sem, sem, at(c, f)).wait_recv()

    def drain(ref, sem):
        remote(ref, ref, sem, sem, at(c, f)).wait_send()

    def up(me, d, n):
        return lax.rem(me + d, n)

    def down(me, d, n):
        return lax.rem(me + n - d, n)

    def at(cc, ff):
        return {"coarse": cc, "fine": ff}

    def cols_of(pair):
        return pl.ds(pl.multiple_of(pair * PAIR, PAIR), PAIR)

    def side_of(which):
        return pl.ds(pl.multiple_of(which * wide, PAIR), wide)

    def loop(start, stop, body):
        def step(d, carry):
            body(d)
            return carry
        lax.fori_loop(start, stop, step, 0)

    def loop_two(start, stop, work, save):
        def step(i, carry):
            d = start + 2 * i
            first, second = work(d), work(d + 1)
            save(d, first)
            save(d + 1, second)
            return carry
        lax.fori_loop(0, (stop - start) // 2, step, 0)
        if (stop - start) % 2:
            save(stop - 1, work(stop - 1))

    def begin(copies):
        for copy in copies:
            copy.start()

    def begin_if(cond, copies):
        @pl.when(cond)
        def _():
            begin(copies)

    loads = [
        pltpu.make_async_copy(enc, encbuf.at[me_kv, me_q], load_s.at[0]),
        pltpu.make_async_copy(kh.at[:, cols_of(p)], kvbuf.at[c, f, 0], load_s.at[1]),
        pltpu.make_async_copy(vh.at[:, cols_of(p)], kvbuf.at[c, f, 1], load_s.at[1]),
        pltpu.make_async_copy(qh.at[:, cols_of(p)], qbuf.at[p], load_s.at[2]),
        pltpu.make_async_copy(decq.at[c, g], drows, load_s.at[3]),
        pltpu.make_async_copy(kl.at[:, side_of(lo)], lk.at[1 + lo], load_s.at[4]),
        pltpu.make_async_copy(vl.at[:, side_of(lo)], lv.at[1 + lo], load_s.at[4]),
        pltpu.make_async_copy(ql.at[:, side_of(lo)], lq.at[lo], load_s.at[5]),
    ]
    for copy in loads:
        copy.start()

    barrier = pltpu.get_barrier_semaphore()

    has_up = me_q < n_q - 1
    has_down = me_q > 0
    n_near = n_coarse + has_up.astype(jnp.int32) + has_down.astype(jnp.int32)

    def greet(sem):
        def say(device):
            pl.semaphore_signal(sem, inc=1, device_id=device, device_id_type=MESH)

        say(at(c, f + 1 - 2 * lo))
        for e in range(1, n_coarse):
            say(at(up(c, e, n_coarse), f))

        @pl.when(has_up)
        def _():
            say(at(c, jnp.minimum(f + LOW, n_fine - 1)))

        @pl.when(has_down)
        def _():
            say(at(c, jnp.maximum(f - LOW, 0)))

    greet(barrier)
    pl.semaphore_wait(barrier, n_near)

    def round_out(r):
        greet(far_s.at[r])

    def round_in(r):
        pl.semaphore_wait(far_s.at[r], n_near)

    def enc_row(way):
        peer = jnp.clip(me_q + way, 0, n_q - 1)
        return remote(
            enc, encbuf.at[me_kv, me_q], enc_s, enc_r.at[me_q], at(c, peer * LOW + lo)
        )

    def enc_mate(block):
        part = encbuf.at[me_kv, block]
        return remote(part, part, ey_s, enc_r.at[n_q + block], at(c, f + 1 - 2 * lo))

    def enc_across(low, block, e):
        part = encbuf.at[c * LOW + low, block]
        return remote(part, part, ex_s, enc_r.at[2 * n_q], at(up(c, e, n_coarse), f))

    def enc_out(block):
        enc_mate(block).start()
        for e in range(1, n_coarse):
            enc_across(lo, block, e).start()

    def enc_at(t):
        for way in (t, -t):
            row = me_q + way
            yield way, jnp.clip(row, 0, n_q - 1), (row >= 0) & (row < n_q)

    def enc_rows(t):
        for way, row, there in enc_at(t):
            begin_if(there, (enc_row(way),))

    def enc_step(t):
        for way, row, there in enc_at(t):
            @pl.when(there)
            def _():
                take(encbuf.at[me_kv, row], enc_r.at[row])
                enc_out(row)

    def enc_turn(block):
        take(encbuf.at[c * LOW + 1 - lo, block], enc_r.at[n_q + block])
        for e in range(1, n_coarse):
            enc_across(1 - lo, block, e).start()

    def enc_side(t):
        for way, row, there in enc_at(t):
            @pl.when(there)
            def _():
                enc_turn(row)

    def q_copy(d):
        to = flip(p, d, pairs)
        return remote(qh.at[:, cols_of(to)], qbuf.at[p], q_s, q_r.at[int(d >= pairs // 2)], at(c, to * share + s_me))

    def kv_copy(d):
        to = flip(f, d, n_fine)
        col = cols_of(lax.div(to, share))
        return (
            remote(kh.at[:, col], kvbuf.at[c, f, 0], kv_s, kv_r.at[f], at(c, to)),
            remote(vh.at[:, col], kvbuf.at[c, f, 1], kv_s, kv_r.at[f], at(c, to)),
        )

    def kv_forward(d):
        src = flip(f, d, n_fine)
        block = kvbuf.at[c, src]
        if d:
            take(block, kv_r.at[src])
        for e in range(1, n_coarse):
            remote(block, block, kx_s, kv_r.at[n_fine + int(d >= half)], at(up(c, e, n_coarse), f)).start()

    def kv_others(far_half):
        take(kvbuf.at[pl.ds(0, n_coarse - 1), pl.ds(0, half)], kv_r.at[n_fine + far_half])

    def o_copy(d):
        to = flip(p, d, pairs)
        return remote(osend.at[to], orecv.at[p], o_s, o_r, at(c, to * share + s_me))

    mate = at(c, f + 1 - 2 * lo)

    def swap_copy():
        cols = side_of(1 - lo)
        return (
            remote(kl.at[:, cols], lk.at[1 + lo], x_s, x_r.at[0], mate),
            remote(vl.at[:, cols], lv.at[1 + lo], x_s, x_r.at[0], mate),
            remote(ql.at[:, cols], lq.at[lo], x_s, x_r.at[1], mate),
        )

    def halo_copy(side):
        peer = jnp.clip(two + 2 * side - 1, 0, n_pair_seq - 1) * LOW + lo
        device = at(lax.div(peer, n_fine), lax.rem(peer, n_fine))
        slot = 3 - 3 * side
        return (
            remote(lk.at[1 + side], lk.at[slot], h_s.at[side], h_r.at[side], device),
            remote(lv.at[1 + side], lv.at[slot], h_s.at[side], h_r.at[side], device),
        )

    has_peer = [two > 0, two < n_pair_seq - 1]
    at_edge = [me_q == 0, me_q == n_q - 1]

    def hop_copy(side):
        peer = jnp.clip(c + 2 * side - 1, 0, n_coarse - 1)
        return remote(lv.at[1 + side], hop, h_s.at[side], hop_r, at(peer, f))

    def hop_on(side):
        end = (1 - side) * (n_q - 1)
        slot = 3 - 3 * side
        return remote(hop, lv.at[slot], hop_s, h_r.at[side], at(c, end * LOW + lo))

    hops_here = [at_edge[0] & (c < n_coarse - 1), at_edge[1] & (c > 0)]

    def halo_send(side, mine):
        go = mine & has_peer[side]
        keys, values = halo_copy(side)

        @pl.when(go)
        def _():
            keys.start()

        @pl.when(go & jnp.logical_not(at_edge[side]))
        def _():
            values.start()

        @pl.when(go & at_edge[side])
        def _():
            hop_copy(side).start()

    def hop_forward():
        for side in range(2):
            @pl.when(hops_here[side])
            def _():
                hop_copy(side).wait_recv()
                hop_on(side).start()

    def light_back(j):
        return remote(lsend.at[j], lrecv.at[j], lo_s, lo_r, mate)

    bits = []
    bit = half // 2
    while bit:
        bits.append(bit)
        bit //= 2

    def dec_copy(block, k):
        mine = dec.at[c, block]
        if k < len(bits):
            peer = at(c, hh * half + flip(g, bits[k], half))
        else:
            peer = at(up(c, k - len(bits) + 1, n_coarse), f)
        return remote(mine, mine, dec_s.at[k], dec_r.at[block if k < len(bits) else half], peer)

    def dec_spread(block, first):
        for k in range(first, len(bits)):
            dec_copy(block, k).start()

    def dec_across(block):
        for k in range(len(bits), len(bits) + n_coarse - 1):
            dec_copy(block, k).start()

    def dec_wave(steps):
        for x in range(1, half):
            if bin(x).count("1") == steps:
                block = flip(g, x, half)
                last = bits.index(x & -x)
                take(dec.at[c, block], dec_r.at[block])
                dec_spread(block, last + 1)
                dec_across(block)

    def q_of(d):
        return (q_copy(d // share),) if d % share == 0 else ()

    def rows_next(d):
        return jnp.abs(lax.div(flip(f, d, n_fine), LOW) - me_q) == 1

    even_near, even_far = range(2, half, 2), range(half, n_fine, 2)
    odd_near, odd_far = range(3, half, 2), range(half + 1, n_fine, 2)
    even = [*even_near, *even_far]

    round_out(1)
    enc_rows(1)
    loads[0].wait()
    enc_out(me_q)
    for d in even:
        begin_if(rows_next(d), q_of(d))
    begin(q_of(1))
    pltpu.make_async_copy(kvbuf.at[c, f], kvbuf.at[c, f], load_s.at[1]).wait()
    kv_forward(0)
    for d in even:
        begin_if(rows_next(d), kv_copy(d))
    begin(kv_copy(1))
    row = lax.broadcasted_iota(jnp.int32, (tokens, 3 * tokens), 0)
    col = lax.broadcasted_iota(jnp.int32, (tokens, 3 * tokens), 1)
    for b in range(LOW):
        pos = (two * LOW + b) * tokens + col - tokens
        seen = (jnp.abs(col - tokens - row) <= ROUTED_BLOCK - 1) & (pos >= 0) & (pos < n_seq * tokens)
        band[b] = jnp.where(seen, jnp.float32(0), jnp.float32(NEG))

    loads[4].wait()
    lane_d = lax.broadcasted_iota(jnp.int32, (dec_rows, PAIR), 1)
    for j in range(pairs):
        q = drows[:, j * PAIR:(j + 1) * PAIR].astype(jnp.float32) * (HEAD ** (-0.5))
        swapped = pltpu.roll(q, HEAD, 1)
        both = jnp.concatenate(
            [jnp.where(lane_d < HEAD, q, 0.0), jnp.where(lane_d < HEAD, swapped, 0.0)], axis=0
        )
        dq[2 * j * dec_rows:(2 * j + 2) * dec_rows, :] = both.astype(jnp.bfloat16)

    for r in range(1, n_q - 1):
        round_in(r)
        round_out(r + 1)
    enc_step(1)
    round_in(n_q - 1)
    for t in range(2, n_q):
        enc_rows(t)
    for d in [*odd_near, *even]:
        begin_if(jnp.logical_not(rows_next(d)) if d % 2 == 0 else here >= 0, q_of(d))
    for d in odd_far:
        begin(q_of(d))
    for d in odd_near:
        begin(kv_copy(d))
    enc_turn(me_q)
    enc_side(1)
    for d in even:
        begin_if(jnp.logical_not(rows_next(d)), kv_copy(d))
    for d in range(2, half, 2):
        kv_forward(d)
    for d in range(1, half, 2):
        kv_forward(d)
    for t in range(2, n_q):
        enc_step(t)
    for d in odd_far:
        begin(kv_copy(d))
    begin(swap_copy())
    far = [*range(half, n_fine, 2), *range(half + 1, n_fine, 2)]
    quarter = len(far) // 4
    d_total = heads * dec_rows
    d_chunk = min(256, d_total)

    def dec_step(i):
        rows = pl.ds(pl.multiple_of(i * d_chunk, d_chunk), d_chunk)
        kv = encbuf[...].reshape(n_seq * tokens, PAIR)
        s = dot_t(dq[rows, :], kv)
        e = jnp.exp(s - jnp.max(s, axis=1, keepdims=True))
        total = jnp.sum(e, axis=1, keepdims=True)
        do[rows, :] = dot(e.astype(jnp.bfloat16), kv) / total

    low_half = lax.broadcasted_iota(jnp.int32, (tokens, PAIR), 1) < HEAD
    lane_2 = lax.broadcasted_iota(jnp.int32, (2 * tokens, PAIR), 1)
    keys = n_coarse * half * tokens

    def heavy_scores(j, part):
        q = stacked_pair(qbuf[j], low_half)
        s = dot_t(q, kvbuf[:, pl.ds(part * half, half), 0].reshape(keys, PAIR))
        if has_bias:
            s = s + bias_ref[part, 0:1, :]
        return s

    def heavy_values(part):
        return kvbuf[:, pl.ds(part * half, half), 1].reshape(keys, PAIR)

    def heavy_first(d):
        j = flip(p, d, pairs)
        s = heavy_scores(j, hh)
        peak = jnp.max(s, axis=1, keepdims=True)
        e = jnp.exp(s - peak)
        total = jnp.sum(e, axis=1, keepdims=True)
        return j, dot(e.astype(jnp.bfloat16), heavy_values(hh)), peak, total

    def heavy_keep(d, result):
        j, o, peak, total = result
        acc[j] = o
        stat[j] = jnp.where(lane_2 == 0, peak, total)

    def heavy_more(d, cc):
        j = flip(p, d, pairs)
        part = 1 - hh
        s = dot_t(stacked_pair(qbuf[j], low_half), kvbuf[cc, pl.ds(part * half, half), 0].reshape(half * tokens, PAIR))
        if has_bias:
            s = s + bias_ref[part, 0:1, pl.ds(pl.multiple_of(cc * half * tokens, PAIR), half * tokens)]
        before = stat[j, :, 0:1]
        peak = jnp.maximum(before, jnp.max(s, axis=1, keepdims=True))
        e = jnp.exp(s - peak)
        keep = jnp.exp(before - peak)
        total = stat[j, :, 1:2] * keep + jnp.sum(e, axis=1, keepdims=True)
        values = kvbuf[cc, pl.ds(part * half, half), 1].reshape(half * tokens, PAIR)
        return j, acc[j] * keep + dot(e.astype(jnp.bfloat16), values), peak, total

    def heavy_last(d, cc):
        j, o, peak, total = heavy_more(d, cc)
        o = o / total
        return j, jnp.where(low_half, o[:tokens], o[tokens:]).astype(jnp.bfloat16)

    loads[3].wait()
    take(qbuf.at[pl.ds(0, pairs // 2 - 1)], q_r.at[0])
    kv_others(0)
    loop_two(0, pairs // 2, heavy_first, heavy_keep)
    for t in range(2, n_q):
        enc_side(t)
    n_chunk = d_total // d_chunk
    n_chunk = d_total // d_chunk
    take(qbuf.at[pl.ds(0, pairs // 2)], q_r.at[1])
    loop_two(pairs // 2, pairs, heavy_first, heavy_keep)
    for d in far[0 * quarter:1 * quarter]:
        kv_forward(d)
    take(encbuf.at[pl.ds(0, LOW * (n_coarse - 1))], enc_r.at[2 * n_q])
    pltpu.make_async_copy(lk.at[pl.ds(0, 2)], lk.at[pl.ds(0, 2)], load_s.at[4]).wait()
    for side in range(2):
        halo_send(side, lo == side)
    loop(0 * n_chunk // 4, 1 * n_chunk // 4, dec_step)
    for d in far[1 * quarter:2 * quarter]:
        kv_forward(d)
    loop(1 * n_chunk // 4, 2 * n_chunk // 4, dec_step)
    for d in far[2 * quarter:3 * quarter]:
        kv_forward(d)
    loop(2 * n_chunk // 4, 3 * n_chunk // 4, dec_step)
    for d in far[3 * quarter:4 * quarter]:
        kv_forward(d)
    loop(3 * n_chunk // 4, n_chunk, dec_step)
    for j in range(pairs):
        even = do[2 * j * dec_rows:(2 * j + 1) * dec_rows, :]
        odd = do[(2 * j + 1) * dec_rows:(2 * j + 2) * dec_rows, :]
        dec[c, g, :, j * PAIR:(j + 1) * PAIR] = jnp.where(
            lane_d < HEAD, pltpu.roll(even, HEAD, 1), odd
        ).astype(jnp.bfloat16)
    dec_spread(g, 0)
    take(lk.at[pl.ds(0, 2)], x_r.at[0])
    for side in range(2):
        halo_send(side, lo == 1 - side)
    dec_across(g)
    loop_two(0, pairs, lambda d: heavy_more(d, c), heavy_keep)
    hop_forward()
    kv_others(1)
    for e in range(1, n_coarse - 1):
        loop_two(0, pairs, lambda d: heavy_more(d, up(c, e, n_coarse)), heavy_keep)

    def heavy_end(i):
        return heavy_last(pairs - 1 - i, up(c, n_coarse - 1, n_coarse))

    def heavy_out(i, result):
        osend[result[0]] = result[1]
        o_copy(pairs - 1 - i).start()

    loop_two(0, pairs // 2, heavy_end, heavy_out)
    dec_wave(1)
    loop_two(pairs // 2, pairs - 2, heavy_end, heavy_out)
    near, home = heavy_end(pairs - 2), heavy_end(pairs - 1)
    heavy_out(pairs - 2, near)
    orecv[p] = home[1]

    take(lq.at[1 - lo], x_r.at[1])
    loads[7].wait()
    for side in range(2):
        @pl.when(has_peer[side])
        def _():
            take(lk.at[pl.ds(0, 2)], h_r.at[1 - side])

        @pl.when(jnp.logical_not(has_peer[side]))
        def _():
            lk[3 * side] = jnp.zeros((tokens, wide), jnp.bfloat16)
            lv[3 * side] = jnp.zeros((tokens, wide), jnp.bfloat16)

    def light_of(b, j):
        cols = cols_of(j)
        q = stacked_pair(lq[b, :, cols], low_half)
        mask = band[b]
        s = dot_t(q, lk[pl.ds(b, 3), :, cols].reshape(3 * tokens, PAIR))
        s = s + jnp.concatenate([mask, mask], axis=0)
        e = jnp.exp(s - jnp.max(s, axis=1, keepdims=True))
        total = jnp.sum(e, axis=1, keepdims=True)
        o = dot(e.astype(jnp.bfloat16), lv[pl.ds(b, 3), :, cols].reshape(3 * tokens, PAIR)) / total
        return jnp.where(low_half, o[:tokens], o[tokens:])

    def light_away(j, o):
        lsend[j] = o.astype(jnp.bfloat16)
        light_back(j).start()

    def light_home(j, o):
        lown[:, cols_of(j)] = o

    loop_two(0, pairs_half, lambda j: light_of(1 - lo, j), light_away)
    for steps in range(2, len(bits) + 1):
        dec_wave(steps)
    loop_two(0, pairs_half, lambda j: light_of(lo, j), light_home)

    take(orecv.at[pl.ds(0, pairs - 1)], o_r)

    def join_home(j):
        pair = lo * pairs_half + j
        heavy = orecv[pair].astype(jnp.float32)
        out[:, cols_of(pair)] = (lown[:, cols_of(j)] + heavy).astype(jnp.bfloat16)

    def join_away(j):
        pair = (1 - lo) * pairs_half + j
        heavy = orecv[pair].astype(jnp.float32)
        out[:, cols_of(pair)] = (lrecv[j].astype(jnp.float32) + heavy).astype(jnp.bfloat16)

    loop(0, pairs_half, join_home)
    take(lrecv, lo_r)
    loop(0, pairs_half, join_away)

    take(dec.at[pl.ds(0, n_coarse - 1)], dec_r.at[half])
    drain(encbuf.at[0, pl.ds(0, n_q - 1)], enc_s)
    drain(encbuf.at[0], ey_s)
    drain(encbuf.at[pl.ds(0, LOW * (n_coarse - 1))], ex_s)
    drain(qbuf.at[pl.ds(0, pairs - 1)], q_s)
    drain(osend.at[pl.ds(0, pairs - 1)], o_s)
    drain(kvbuf.at[0, pl.ds(0, n_fine - 1)], kv_s)
    drain(kvbuf.at[pl.ds(0, n_coarse - 1)], kx_s)
    drain(lk.at[pl.ds(0, 3)], x_s)
    drain(lsend, lo_s)
    for side in range(2):
        @pl.when(has_peer[side])
        def _():
            drain(lk.at[pl.ds(0, 2)], h_s.at[side])

        @pl.when(hops_here[side])
        def _():
            drain(hop, hop_s)
    for k in range(len(bits) + n_coarse - 1):
        drain(dec.at[0, pl.ds(0, min(2 ** k, half))], dec_s.at[k])


def local(
    q_light, k_light, v_light, q_heavy, k_heavy, v_heavy, enc_kv, dec_queries, query_ids, key_ids
):
    _, tokens, width = q_light.shape
    n_coarse = lax.axis_size("coarse")
    n_fine = lax.axis_size("fine")
    n_seq = n_coarse * n_fine
    n_q = n_fine // LOW
    n_kv = n_coarse * LOW
    half = n_fine // 2
    heads = width // HEAD
    pairs = heads // 2
    count = dec_queries.shape[1]
    dec_rows = count // (n_coarse * half)
    n_bits = half.bit_length() - 1
    mine = dec_queries.reshape(n_coarse, half, dec_rows, width)
    args = [q_light[0], k_light[0], v_light[0], q_heavy[0], k_heavy[0], v_heavy[0], enc_kv[0], mine]
    args = [pltpu.with_memory_space_constraint(a, pltpu.HBM) for a in args]
    has_bias = key_ids.shape[1] != n_seq
    keys = n_coarse * half * tokens
    if has_bias:
        blocks = jnp.arange(n_seq, dtype=jnp.int32).reshape(n_coarse, 2, half).transpose(1, 0, 2)
        listed = jnp.any(blocks[..., None] == key_ids[0], axis=-1).reshape(2, 1, n_coarse * half)
        bias = jnp.repeat(jnp.where(listed, 0.0, NEG).astype(jnp.float32), tokens, axis=2)
        args.append(jnp.broadcast_to(bias, (2, 8, keys)))
    bf16, f32 = jnp.bfloat16, jnp.float32
    dma = pltpu.SemaphoreType.DMA
    vmem = pl.BlockSpec(memory_space=pltpu.VMEM)
    hbm = pl.BlockSpec(memory_space=pltpu.HBM)
    wide = width // LOW
    encoded, decoded = pl.pallas_call(
        functools.partial(kernel, (n_coarse, n_fine, tokens, width, dec_rows), has_bias),
        out_shape=(
            jax.ShapeDtypeStruct((tokens, width), bf16),
            jax.ShapeDtypeStruct((n_coarse, half, dec_rows, width), bf16),
        ),
        in_specs=[hbm] * 8 + [vmem] * (len(args) - 8),
        out_specs=(vmem, vmem),
        scratch_shapes=[
            pltpu.VMEM((n_kv, n_q, tokens, PAIR), bf16),
            pltpu.VMEM((dec_rows, width), bf16),
            pltpu.VMEM((heads * dec_rows, PAIR), bf16),
            pltpu.VMEM((heads * dec_rows, PAIR), f32),
            pltpu.VMEM((pairs, tokens, PAIR), bf16),
            pltpu.VMEM((n_coarse, n_fine, 2, tokens, PAIR), bf16),
            pltpu.VMEM((pairs, 2 * tokens, PAIR), f32),
            pltpu.VMEM((pairs, 2 * tokens, PAIR), f32),
            pltpu.VMEM((pairs, tokens, PAIR), bf16),
            pltpu.VMEM((pairs, tokens, PAIR), bf16),
            pltpu.VMEM((2, tokens, wide), bf16),
            pltpu.VMEM((4, tokens, wide), bf16),
            pltpu.VMEM((4, tokens, wide), bf16),
            pltpu.VMEM((tokens, wide), bf16),
            pltpu.VMEM((tokens, wide), f32),
            pltpu.VMEM((pairs // LOW, tokens, PAIR), bf16),
            pltpu.VMEM((pairs // LOW, tokens, PAIR), bf16),
            pltpu.VMEM((2, tokens, 3 * tokens), f32),
            dma((6,)),
            dma, dma((2 * n_q + 1,)), dma, dma,
            dma, dma((2,)),
            dma, dma((n_fine + 2,)), dma,
            pltpu.SemaphoreType.REGULAR((n_q,)),
            dma, dma((2,)),
            dma((2,)), dma((2,)),
            dma, dma,
            dma, dma,
            dma, dma,
            dma((n_bits + n_coarse - 1,)), dma((half + 1,)),
        ],
        compiler_params=pltpu.CompilerParams(
            collective_id=0, has_side_effects=True, vmem_limit_bytes=32 * 1024 * 1024
        ),
    )(*args)
    return encoded[None], decoded.reshape(1, count, width)


def solution(mesh):
    rows = P("doc", ("coarse", "fine"), None)
    placed = (rows,) * 7 + (P("doc", None, None), P("doc", None), P("doc", None))
    return jax.shard_map(
        local,
        mesh=mesh,
        in_specs=placed,
        out_specs=(rows, P("doc", None, None)),
        check_vma=False,
    )
```
